32 devices in a mesh: seq: 4 (over y, core), tp: 4 (over z), dp: 2 (over x).
Axes of the slice: x: 2, y: 2, z: 4, core: 2. Of those that a mesh axis runs over, the one named last changes fastest.
Arguments:
- queries: bfloat16 [2048, 4096], P(('dp', 'seq'), 'tp'), parts along dimension 0, may hold values from -36 to 36
- key_rows: bfloat16 [2048, 4096], P(('dp', 'seq'), 'tp'), parts along dimension 0, may hold values from -36 to 36
- values: bfloat16 [2048, 4096], P(('dp', 'seq'), 'tp'), parts along dimension 0, may hold values from -6 to 6
- modality: int32 [2048], P(('dp', 'seq')), parts along dimension 0, may hold values from 0 to 1, as said below
- out_weight: bfloat16 [2, 4096, 4096], P(None, 'tp'), may hold values from -0.125 to 0.125
Outputs:
- layer_out: bfloat16 [2048, 4096], P(('dp', 'seq'), 'tp'), parts along dimension 0
The draws below stay inside these ranges and needn't reach their ends.
There are 2 independent parts, one for each index of `dp`. The reference program is written for one: setup_inputs(seed, part) draws one part's arguments, and reference() takes and returns one part's arrays. A program takes and returns all parts, laid end to end along the dimension named above; an argument that names none is the same for every part. Nothing has to cross between parts.
Inputs may be any that keep to these rules, and one draw needn't show every extreme that they name: `modality`: 1 marks an image token, 0 a text token.
All inputs are finite; a program needn't handle non-finite values.
Results may differ from the reference program's by a relative error of at most 0.013.
Values may be sent and summed in bfloat16 or wider, within the bound.
No kernel may reach another device: no remote copies, remote signals or barrier semaphores. Data moves between devices by JAX's collectives and lax.ppermute only.
A program may use at most 64 MiB of HBM per device.

```python
import jax
import jax.numpy as jnp
from jax import lax

D = 4096
H = 32
HD = 128
TOK_DEV = 256
TOKENS = 1024
N_TP = 4


def rough_field(key):
    base = jax.random.truncated_normal(jax.random.fold_in(key, 3), -4.0, 4.0, (TOKENS, H * HD), jnp.float32) * 1.5
    return base.astype(jnp.bfloat16)


def draw_queries(key, part):
    return rough_field(jax.random.fold_in(key, 41))


def draw_key_rows(key, part):
    return rough_field(jax.random.fold_in(key, 42))


def draw_modality(key, part):
    span_count = max(2, TOKENS // 512)
    starts = jax.random.randint(jax.random.fold_in(key, 21), (span_count,), 0, TOKENS)
    widths = jax.random.randint(jax.random.fold_in(key, 22), (span_count,), 1, max(2, 2 * TOK_DEV))
    positions = jnp.arange(TOKENS, dtype=jnp.int32)
    inside = (positions[:, None] >= starts[None, :]) & (positions[:, None] < starts[None, :] + widths[None, :])
    return jnp.any(inside, axis=1).astype(jnp.int32)


def strengthened(result, rng, source, target, blocks, factor):
    def block_of(axis_at):
        return (jnp.arange(result.shape[axis_at]) // (result.shape[axis_at] // blocks)).reshape((-1,) + (1,) * (result.ndim - 1 - axis_at))

    one_side = jax.random.permutation(rng, blocks)[block_of(target)]
    far = (block_of(target) + blocks // 2) % blocks
    return jnp.where((block_of(source) == one_side) | (block_of(source) == far), factor * result, result)


def shard_levels(stream_key, extent, shards, smallest, high):
    gain = 1.0
    for position, shards_of in shards:
        draws = jax.random.uniform(jax.random.fold_in(jax.random.fold_in(stream_key, 6), position), (shards_of,), jnp.float32, smallest / len(shards), high / len(shards))
        gain = gain * jnp.repeat(jnp.exp(draws), extent[position] // shards_of).reshape((-1,) + (1,) * (len(extent) - 1 - position))
    return gain


def centred(rng, extent, spread, limit, pieces=(), held_as=jnp.bfloat16):
    level = shard_levels(rng, extent, pieces, -0.22, 0.18) if pieces else 1.0
    entries = jax.random.normal(rng, extent, jnp.float32) * spread * level
    return jnp.minimum(jnp.maximum(entries, -limit), limit).astype(held_as)


def bell_draw_with(stream_key, extent, spread, bound, pieces, heavy, held_as=jnp.bfloat16):
    result = spread * jax.random.normal(stream_key, extent, jnp.float32)
    if pieces:
        result = result * shard_levels(stream_key, extent, pieces, -0.22, 0.18)
    return jnp.clip(strengthened(result, jax.random.fold_in(stream_key, 3), *heavy), -bound, bound).astype(held_as)


def setup_inputs(seed: int = 0, part: int = 0) -> dict:
    splits = jax.random.split(jax.random.key(seed), 6)
    part_keys = jax.random.split(jax.random.fold_in(splits[5], part), 6)
    queries = draw_queries(jax.random.fold_in(jax.random.fold_in(splits[5], part), 71), part)
    key_rows = draw_key_rows(jax.random.fold_in(jax.random.fold_in(splits[5], part), 71), part)
    values = centred(part_keys[2], (TOKENS, H * HD), 1.0, 6.0, ((0, 4), (1, 4)))
    modality = draw_modality(jax.random.fold_in(jax.random.fold_in(splits[5], part), 71), part)
    out_weight = bell_draw_with(splits[4], (2, H * HD, D), (H * HD) ** -0.5, 0.125, ((1, 4),), (1, 2, 4, 2.0))
    return dict(queries=queries, key_rows=key_rows, values=values, modality=modality, out_weight=out_weight)


def split_heads(field):
    return field.reshape(TOKENS, H, HD).transpose(1, 0, 2)


def reference(queries, key_rows, values, modality, out_weight):
    score_scale = HD ** -0.5
    positions = jnp.arange(TOKENS, dtype=jnp.int32)
    allowed = positions[:, None] >= positions[None, :]

    def one_head(inputs):
        query_head, key_head, value_head = inputs
        scores = jnp.dot(query_head, key_head.T, preferred_element_type=jnp.float32) * score_scale
        scores = jnp.where(allowed, scores, -jnp.inf)
        largest = jnp.max(scores, axis=1, keepdims=True)
        weights = jnp.exp(scores - largest)
        probabilities = (weights / jnp.sum(weights, axis=1, keepdims=True)).astype(jnp.bfloat16)
        return jnp.dot(probabilities, value_head, preferred_element_type=jnp.float32).astype(jnp.bfloat16)

    attended = lax.map(one_head, (split_heads(queries), split_heads(key_rows), split_heads(values)))
    attended = attended.transpose(1, 0, 2).reshape(TOKENS, H * HD)
    shard_cols = (H // N_TP) * HD
    image_rows = modality[:, None] == 1
    total = jnp.zeros((TOKENS, D), jnp.float32)
    for shard_index in range(N_TP):
        lower = shard_index * shard_cols
        piece = attended[:, lower:lower + shard_cols]
        text_part = jnp.dot(piece, out_weight[0, lower:lower + shard_cols], preferred_element_type=jnp.float32)
        image_part = jnp.dot(piece, out_weight[1, lower:lower + shard_cols], preferred_element_type=jnp.float32)
        partial_value = jnp.where(image_rows, image_part, text_part).astype(jnp.bfloat16)
        total = total + partial_value.astype(jnp.float32)
    return total.astype(jnp.bfloat16)
```

```python
import functools

import jax
import jax.numpy as jnp
import numpy as np
from jax import lax
from jax.experimental import pallas as pl
from jax.experimental.pallas import tpu as pltpu
from jax.sharding import PartitionSpec as P

HD = 128
LANES = 128
PARTS = 2
LOG2E = float(np.log2(np.e))
LSE_STEP = 32


def params(mib):
    return pltpu.CompilerParams(vmem_limit_bytes=mib * 1024 * 1024)


def softmax_rows(query, keys, values, masks, scale):
    scores = []
    for key, mask in zip(keys, masks):
        s = lax.dot_general(query, key, (((1,), (1,)), ((), ())), preferred_element_type=jnp.float32)
        scores.append(s if mask is None else jnp.where(mask, s, -jnp.inf))
    largest = functools.reduce(jnp.maximum, [jnp.max(s, axis=1, keepdims=True) for s in scores])
    total = None
    for s, value in zip(scores, values):
        weights = jnp.exp2((s - largest) * (scale * LOG2E)).astype(jnp.bfloat16)
        ones = jnp.ones((value.shape[0], LANES), jnp.bfloat16)
        part = jnp.dot(weights, jnp.concatenate([value, ones], axis=1), preferred_element_type=jnp.float32)
        total = part if total is None else total + part
    head = value.shape[1]
    sums = total[:, head : head + LANES]
    return total[:, :head] / sums, largest * (scale * LOG2E) + jnp.log2(sums[:, :1])


def own_kernel(offsets, place_ref, q_ref, *refs):
    count = len(offsets)
    k_refs, v_refs = refs[:count], refs[count : 2 * count]
    out_ref, lse_ref = refs[2 * count :]
    me = place_ref[0]
    rows = q_ref.shape[0]
    scale = HD**-0.5
    below = lax.broadcasted_iota(jnp.int32, (rows, rows), 0) >= lax.broadcasted_iota(jnp.int32, (rows, rows), 1)
    masks = [below if o == 0 else lax.broadcast(jnp.bitwise_xor(me, o), (rows, rows)) < me for o in offsets]
    for h in range(q_ref.shape[1] // HD):
        at = slice(h * HD, (h + 1) * HD)
        result, lse = softmax_rows(q_ref[:, at], [k[:, at] for k in k_refs], [v[:, at] for v in v_refs], masks, scale)
        out_ref[:, at] = result.astype(out_ref.dtype)
        lse_ref[:, h : h + 1] = lse


def cross_kernel(count, half, place_ref, q_ref, *refs):
    k_refs, v_refs = refs[:count], refs[count : 2 * count]
    (out_ref,) = refs[2 * count :]
    scale = HD**-0.5
    width = q_ref.shape[1]

    @pl.when(place_ref[0] < half)
    def _():
        out_ref[:, width:] = jnp.zeros((out_ref.shape[0], out_ref.shape[1] - width), out_ref.dtype)
        for h in range(width // HD):
            at = slice(h * HD, (h + 1) * HD)
            result, lse = softmax_rows(
                q_ref[:, at], [k[:, at] for k in k_refs], [v[:, at] for v in v_refs], [None] * count, scale
            )
            out_ref[:, at] = result.astype(out_ref.dtype)
            for step in range(3):
                piece = lse.astype(jnp.bfloat16)
                col = width + step * LSE_STEP + h
                out_ref[:, col : col + 1] = piece
                lse = lse - piece.astype(jnp.float32)


def merge_kernel(half, place_ref, own_ref, lse_ref, far_ref, kinds_ref, w_ref, att_ref, out_ref):
    width = own_ref.shape[1]
    step = pl.program_id(0)

    @pl.when(step == 0)
    def _():
        upper = place_ref[0] >= half
        for h in range(width // HD):
            at = slice(h * HD, (h + 1) * HD)
            far_lse = sum(
                far_ref[:, width + i * LSE_STEP + h : width + i * LSE_STEP + h + 1].astype(jnp.float32) for i in range(3)
            )
            mine = 1.0 / (1.0 + jnp.exp2(far_lse - lse_ref[:, h : h + 1]))
            mine = jnp.where(upper, mine, 1.0)
            mixed = own_ref[:, at].astype(jnp.float32) * mine + far_ref[:, at].astype(jnp.float32) * (1.0 - mine)
            att_ref[:, at] = mixed.astype(att_ref.dtype)

    project(att_ref, kinds_ref, w_ref, out_ref)


def project(att_ref, kinds_ref, w_ref, out_ref):
    rows = att_ref[...]
    image = kinds_ref[...] == 1
    nothing = jnp.zeros_like(rows)
    total = jnp.dot(jnp.where(image, nothing, rows), w_ref[0], preferred_element_type=jnp.float32)
    total += jnp.dot(jnp.where(image, rows, nothing), w_ref[1], preferred_element_type=jnp.float32)
    out_ref[...] = total.astype(out_ref.dtype)


def project_kernel(place_ref, att_ref, kinds_ref, w_ref, out_ref):
    project(att_ref, kinds_ref, w_ref, out_ref)


def on_device(queries, key_rows, values, modality, out_weight):
    seq_count = lax.axis_size("seq")
    tp_count = lax.axis_size("tp")
    half = seq_count // 2
    place = jnp.stack([lax.axis_index("seq"), lax.axis_index("tp")]).astype(jnp.int32)
    rows, width = queries.shape
    part_rows = rows // PARTS
    model = out_weight.shape[2]
    chunk = model // tp_count
    block = min(chunk, 256)
    steps = chunk // block
    kinds = modality.reshape(rows, 1)
    vmem = pl.BlockSpec(memory_space=pltpu.VMEM)
    smem = pl.BlockSpec(memory_space=pltpu.SMEM)

    def xor(count, bit):
        return [(i, i ^ bit) for i in range(count)]

    far_queries = [
        lax.ppermute(queries[p * part_rows : (p + 1) * part_rows], "seq", [(i + half, i) for i in range(half)])
        for p in range(PARTS)
    ]

    offsets, keys, vals = [0], [key_rows], [values]
    bit = half // 2
    while bit:
        keys = keys + [lax.ppermute(x, "seq", xor(seq_count, bit)) for x in keys]
        vals = vals + [lax.ppermute(x, "seq", xor(seq_count, bit)) for x in vals]
        offsets = offsets + [o ^ bit for o in offsets]
        bit //= 2
    count = len(offsets)

    own, own_lse = pl.pallas_call(
        functools.partial(own_kernel, tuple(offsets)),
        out_shape=(
            jax.ShapeDtypeStruct((rows, width), jnp.bfloat16),
            jax.ShapeDtypeStruct((rows, LANES), jnp.float32),
        ),
        in_specs=[smem] + [vmem] * (1 + 2 * count),
        out_specs=(vmem, vmem),
        compiler_params=params(24),
        name="own",
    )(place, queries, *keys, *vals)

    cross = pl.pallas_call(
        functools.partial(cross_kernel, count, half),
        out_shape=jax.ShapeDtypeStruct((part_rows, width + LANES), jnp.bfloat16),
        in_specs=[smem] + [vmem] * (1 + 2 * count),
        out_specs=vmem,
        compiler_params=params(24),
        name="cross",
    )
    far = [
        lax.ppermute(cross(place, q, *keys, *vals), "seq", [(i, i + half) for i in range(half)]) for q in far_queries
    ]

    def weight_spec(offset):
        return pl.BlockSpec(
            (2, width, block), lambda i, place: (0, 0, jnp.bitwise_xor(place[1], offset) * steps + i)
        )

    whole = lambda *_: (0, 0)

    def merged(p, offset):
        here = lambda *_: (p, 0)
        return pl.pallas_call(
            functools.partial(merge_kernel, half),
            out_shape=(
                jax.ShapeDtypeStruct((part_rows, width), jnp.bfloat16),
                jax.ShapeDtypeStruct((part_rows, chunk), jnp.bfloat16),
            ),
            grid_spec=pltpu.PrefetchScalarGridSpec(
                num_scalar_prefetch=1,
                grid=(steps,),
                in_specs=[
                    pl.BlockSpec((part_rows, width), here),
                    pl.BlockSpec((part_rows, LANES), here),
                    pl.BlockSpec((part_rows, width + LANES), whole),
                    pl.BlockSpec((part_rows, 1), here),
                    weight_spec(offset),
                ],
                out_specs=(
                    pl.BlockSpec((part_rows, width), whole),
                    pl.BlockSpec((part_rows, block), lambda i, place: (0, i)),
                ),
            ),
            compiler_params=params(24),
            name="merge",
        )(place, own, own_lse, far[p], kinds, out_weight)

    def projected(p, attended, offset):
        here = lambda *_: (p, 0)
        return pl.pallas_call(
            project_kernel,
            out_shape=jax.ShapeDtypeStruct((part_rows, chunk), jnp.bfloat16),
            grid_spec=pltpu.PrefetchScalarGridSpec(
                num_scalar_prefetch=1,
                grid=(steps,),
                in_specs=[
                    pl.BlockSpec((part_rows, width), whole),
                    pl.BlockSpec((part_rows, 1), here),
                    weight_spec(offset),
                ],
                out_specs=pl.BlockSpec((part_rows, block), lambda i, place: (0, i)),
            ),
            compiler_params=params(24),
            name="project",
        )(place, attended, kinds, out_weight)

    def add(*terms):
        return sum(x.astype(jnp.float32) for x in terms)

    results = []
    for p in range(PARTS):
        attended, first = merged(p, tp_count - 1)
        have = {tp_count - 1: first}
        for offset in range(tp_count - 1):
            have[offset] = projected(p, attended, offset)
        bit = 1
        while bit < tp_count:
            keep = {}
            for offset in sorted(have, reverse=True):
                if offset & bit:
                    arrived = lax.ppermute(have[offset], "tp", xor(tp_count, bit))
                    keep[offset ^ bit] = add(have[offset ^ bit], arrived)
            have = {o: x.astype(jnp.bfloat16) for o, x in keep.items()}
            bit *= 2
        results.append(have[0])
    return jnp.concatenate(results, axis=0)


def solution(mesh):
    in_specs = (
        P(("dp", "seq"), "tp"),
        P(("dp", "seq"), "tp"),
        P(("dp", "seq"), "tp"),
        P(("dp", "seq")),
        P(None, "tp", None),
    )
    out_specs = P(("dp", "seq"), "tp")
    return jax.shard_map(on_device, mesh=mesh, in_specs=in_specs, out_specs=out_specs, check_vma=False)
```

```python
import functools

import jax
import jax.numpy as jnp
import numpy as np
from jax import lax
from jax.experimental import pallas as pl
from jax.experimental.pallas import tpu as pltpu
from jax.sharding import PartitionSpec as P


HD = 128
LANES = 128
SHARES = (1, 2)
BLOCK = 256
LOG2E = float(np.log2(np.e))
LSE_STEP = 32


def params(mib):
    return pltpu.CompilerParams(vmem_limit_bytes=mib * 1024 * 1024)


def in_hbm(x):
    return pltpu.with_memory_space_constraint(x, pltpu.HBM)


def softmax_rows(query, keys, values, masks, scale):
    scores = []
    for key, mask in zip(keys, masks):
        s = lax.dot_general(query, key, (((1,), (1,)), ((), ())), preferred_element_type=jnp.float32)
        scores.append(s if mask is None else jnp.where(mask, s, -jnp.inf))
    largest = functools.reduce(jnp.maximum, [jnp.max(s, axis=1, keepdims=True) for s in scores])
    total = None
    for s, value in zip(scores, values):
        weights = jnp.exp2((s - largest) * (scale * LOG2E)).astype(jnp.bfloat16)
        ones = jnp.ones((value.shape[0], LANES), jnp.bfloat16)
        part = jnp.dot(weights, jnp.concatenate([value, ones], axis=1), preferred_element_type=jnp.float32)
        total = part if total is None else total + part
    head = value.shape[1]
    sums = total[:, head : head + LANES]
    return total[:, :head] / sums, largest * (scale * LOG2E) + jnp.log2(sums[:, :1])


def column_copies(place_ref, offsets, w_hbm, w_ref, sems, first):
    chunk = w_ref.shape[2] // len(offsets)
    copies = []
    for i, offset in enumerate(offsets):
        start = pl.multiple_of(jnp.bitwise_xor(place_ref[1], offset) * chunk, chunk)
        src, dst = w_hbm.at[:, :, pl.ds(start, chunk)], w_ref.at[:, :, pl.ds(i * chunk, chunk)]
        copies.append(pltpu.make_async_copy(src, dst, sems.at[first + i]))
    return copies


def own_kernel(offsets, loads, place_ref, kinds_ref, q_hbm, k_hbm, v_hbm, w_hbm, *refs):
    others = len(offsets) - 1
    k_refs, v_refs = refs[:others], refs[others : 2 * others]
    out_ref, lse_ref, k_ref, v_ref, columns_ref, w_ref, q_ref, sems = refs[2 * others :]
    pairs = [(q_hbm, q_ref), (k_hbm, k_ref), (v_hbm, v_ref)]
    copies = [pltpu.make_async_copy(src, dst, sems.at[i]) for i, (src, dst) in enumerate(pairs)]
    later = column_copies(place_ref, loads, w_hbm, w_ref, sems, len(pairs))
    for copy in copies + later:
        copy.start()
    me = place_ref[0]
    rows = q_ref.shape[0]
    columns_ref[...] = jnp.broadcast_to(kinds_ref[...].astype(jnp.float32), (LANES, rows)).T
    for copy in copies:
        copy.wait()
    below = lax.broadcasted_iota(jnp.int32, (rows, rows), 0) >= lax.broadcasted_iota(jnp.int32, (rows, rows), 1)
    masks = [below if o == 0 else lax.broadcast(jnp.bitwise_xor(me, o), (rows, rows)) < me for o in offsets]
    for h in range(q_ref.shape[1] // HD):
        at = slice(h * HD, (h + 1) * HD)
        keys = [k[:, at] for k in (k_ref, *k_refs)]
        vals = [v[:, at] for v in (v_ref, *v_refs)]
        result, lse = softmax_rows(q_ref[:, at], keys, vals, masks, HD**-0.5)
        out_ref[:, at] = result.astype(out_ref.dtype)
        lse_ref[:, h : h + 1] = lse
    for copy in later:
        copy.wait()


def cross_kernel(count, half, loads, place_ref, q_ref, *refs):
    k_refs, v_refs = refs[:count], refs[count : 2 * count]
    later = []
    if loads:
        w_hbm, out_ref, w_ref, sems = refs[2 * count :]
        later = column_copies(place_ref, loads, w_hbm, w_ref, sems, 0)
    else:
        (out_ref,) = refs[2 * count :]
    for copy in later:
        copy.start()
    width = q_ref.shape[1]

    @pl.when(place_ref[0] < half)
    def _():
        out_ref[:, width:] = jnp.zeros((out_ref.shape[0], out_ref.shape[1] - width), out_ref.dtype)
        for h in range(width // HD):
            at = slice(h * HD, (h + 1) * HD)
            result, lse = softmax_rows(
                q_ref[:, at], [k[:, at] for k in k_refs], [v[:, at] for v in v_refs], [None] * count, HD**-0.5
            )
            out_ref[:, at] = result.astype(out_ref.dtype)
            for step in range(3):
                piece = lse.astype(jnp.bfloat16)
                col = width + step * LSE_STEP + h
                out_ref[:, col : col + 1] = piece
                lse = lse - piece.astype(jnp.float32)

    for copy in later:
        copy.wait()


def project(rows, image, first, w_ref, out_ref):
    chunk = out_ref.shape[1]
    block = min(chunk, BLOCK)
    nothing = jnp.zeros_like(rows)
    text_rows, image_rows = jnp.where(image, nothing, rows), jnp.where(image, rows, nothing)
    for b in range(0, chunk, block):
        at = slice(first + b, first + b + block)
        total = jnp.dot(text_rows, w_ref[0, :, at], preferred_element_type=jnp.float32)
        total += jnp.dot(image_rows, w_ref[1, :, at], preferred_element_type=jnp.float32)
        out_ref[:, b : b + block] = total.astype(out_ref.dtype)


def merge_kernel(half, lo, first, place_ref, own_ref, lse_ref, far_ref, kinds_ref, w_ref, att_ref, out_ref):
    count, width = att_ref.shape
    rows = slice(lo, lo + count)
    upper = place_ref[0] >= half
    for h in range(width // HD):
        at = slice(h * HD, (h + 1) * HD)
        cols = [width + i * LSE_STEP + h for i in range(3)]
        far_lse = sum(far_ref[:, c : c + 1].astype(jnp.float32) for c in cols)
        mine = 1.0 / (1.0 + jnp.exp2(far_lse - lse_ref[rows, h : h + 1]))
        mine = jnp.where(upper, mine, 1.0)
        mixed = own_ref[rows, at].astype(jnp.float32) * mine + far_ref[:, at].astype(jnp.float32) * (1.0 - mine)
        att_ref[:, at] = mixed.astype(att_ref.dtype)
    project(att_ref[...], kinds_ref[rows, :1] == 1, first, w_ref, out_ref)


def project_kernel(lo, first, kinds_ref, w_ref, *refs):
    att_refs, out_ref = refs[:-1], refs[-1]
    rows = jnp.concatenate([x[...] for x in att_refs], axis=0)
    project(rows, kinds_ref[lo : lo + rows.shape[0], :1] == 1, first, w_ref, out_ref)


def on_device(queries, key_rows, values, modality, out_weight):
    seq_count = lax.axis_size("seq")
    tp_count = lax.axis_size("tp")
    half = seq_count // 2
    place = jnp.stack([lax.axis_index("seq"), lax.axis_index("tp")]).astype(jnp.int32)
    rows, width = queries.shape
    chunk = out_weight.shape[2] // tp_count
    vmem = pl.BlockSpec(memory_space=pltpu.VMEM)
    smem = pl.BlockSpec(memory_space=pltpu.SMEM)
    hbm = pl.BlockSpec(memory_space=pltpu.HBM)
    edges = [0, *(rows * share // SHARES[-1] for share in SHARES)]
    parts = list(zip(edges[:-1], edges[1:]))

    def xor(count, bit):
        return [(i, i ^ bit) for i in range(count)]

    order = sorted(range(tp_count), reverse=True)
    early_loads, late_loads = order[: tp_count // 2], order[tp_count // 2 :]

    def columns_shape(loads):
        return jax.ShapeDtypeStruct((out_weight.shape[0], width, chunk * len(loads)), out_weight.dtype)

    offsets, keys, vals = [0], [key_rows], [values]
    bit = half // 2
    while bit:
        keys = keys + [lax.ppermute(x, "seq", xor(seq_count, bit)) for x in keys]
        vals = vals + [lax.ppermute(x, "seq", xor(seq_count, bit)) for x in vals]
        offsets = offsets + [o ^ bit for o in offsets]
        bit //= 2
    count = len(offsets)

    far_queries = []
    for lo, hi in parts:
        far_queries.append(lax.ppermute(queries[lo:hi], "seq", [(i + half, i) for i in range(half)]))

    own, own_lse, keys[0], vals[0], kinds, early = pl.pallas_call(
        functools.partial(own_kernel, tuple(offsets), tuple(early_loads)),
        out_shape=(
            jax.ShapeDtypeStruct((rows, width), jnp.bfloat16),
            jax.ShapeDtypeStruct((rows, LANES), jnp.float32),
            jax.ShapeDtypeStruct(key_rows.shape, key_rows.dtype),
            jax.ShapeDtypeStruct(values.shape, values.dtype),
            jax.ShapeDtypeStruct((rows, LANES), jnp.float32),
            columns_shape(early_loads),
        ),
        in_specs=[smem, vmem] + [hbm] * 4 + [vmem] * (2 * count - 2),
        out_specs=(vmem,) * 6,
        scratch_shapes=[
            pltpu.VMEM(queries.shape, queries.dtype),
            pltpu.SemaphoreType.DMA((3 + len(early_loads),)),
        ],
        compiler_params=params(8),
        name="own",
    )(place, modality.reshape(1, rows), *(in_hbm(x) for x in (queries, key_rows, values, out_weight)), *keys[1:], *vals[1:])

    far = []
    for p, (lo, hi) in enumerate(parts):
        loads = tuple(late_loads) if p == 0 else ()
        found = pl.pallas_call(
            functools.partial(cross_kernel, count, half, loads),
            out_shape=(jax.ShapeDtypeStruct((hi - lo, width + LANES), jnp.bfloat16),)
            + ((columns_shape(loads),) if loads else ()),
            in_specs=[smem] + [vmem] * (1 + 2 * count) + [hbm] * bool(loads),
            out_specs=(vmem,) * (1 + bool(loads)),
            scratch_shapes=[pltpu.SemaphoreType.DMA((len(loads),))] if loads else [],
            compiler_params=params(8),
            name="cross",
        )(place, far_queries[p], *keys, *vals, *((in_hbm(out_weight),) if loads else ()))
        if loads:
            late = found[1]
        found = found[0]
        far.append(lax.ppermute(found, "seq", [(i, i + half) for i in range(half)]))

    def columns_of(offset):
        if offset in early_loads:
            return early, early_loads.index(offset) * chunk
        return late, late_loads.index(offset) * chunk

    def merged(p, offset):
        weight, first = columns_of(offset)
        lo, hi = parts[p]
        return pl.pallas_call(
            functools.partial(merge_kernel, half, lo, first),
            out_shape=(
                jax.ShapeDtypeStruct((hi - lo, width), jnp.bfloat16),
                jax.ShapeDtypeStruct((hi - lo, chunk), jnp.bfloat16),
            ),
            in_specs=[smem] + [vmem] * 5,
            out_specs=(vmem, vmem),
            compiler_params=params(8),
            name="merge",
        )(place, own, own_lse, far[p], kinds, weight)

    def projected(lo, attended, offset):
        weight, first = columns_of(offset)
        return pl.pallas_call(
            functools.partial(project_kernel, lo, first),
            out_shape=jax.ShapeDtypeStruct((sum(x.shape[0] for x in attended), chunk), jnp.bfloat16),
            in_specs=[vmem] * (2 + len(attended)),
            out_specs=vmem,
            compiler_params=params(8),
            name="project",
        )(kinds, weight, *attended)

    def add(*terms):
        return sum(x.astype(jnp.float32) for x in terms)

    attended, sums = [], []
    for p in range(len(parts)):
        here, first = merged(p, tp_count - 1)
        attended.append(here)
        have = {tp_count - 1: first}
        for offset in range(2, tp_count - 1):
            have[offset] = projected(parts[p][0], [here], offset)
        bit, arrivals = 1, []
        while bit < tp_count:
            keep = dict(have)
            for offset in sorted(have, reverse=True):
                if offset & bit:
                    arrived = lax.ppermute(keep.pop(offset), "tp", xor(tp_count, bit))
                    if offset == bit:
                        arrivals.append(arrived)
                    else:
                        keep[offset ^ bit] = add(have[offset ^ bit], arrived).astype(jnp.bfloat16)
            have = keep
            bit *= 2
        sums.append(arrivals)
    beside = projected(0, attended, 1)
    beside = lax.ppermute(beside, "tp", xor(tp_count, 1))
    total = projected(0, attended, 0)
    total = add(total, beside)
    for arrivals in zip(*sums):
        total = add(total, jnp.concatenate(arrivals, axis=0))
    return total.astype(jnp.bfloat16)


def solution(mesh):
    in_specs = (
        P(("dp", "seq"), "tp"),
        P(("dp", "seq"), "tp"),
        P(("dp", "seq"), "tp"),
        P(("dp", "seq")),
        P(None, "tp", None),
    )
    out_specs = P(("dp", "seq"), "tp")

    return jax.shard_map(on_device, mesh=mesh, in_specs=in_specs, out_specs=out_specs, check_vma=False)
```

```python
import functools

import jax
import jax.numpy as jnp
import numpy as np
from jax import lax
from jax.experimental import pallas as pl
from jax.experimental.pallas import tpu as pltpu
from jax.sharding import PartitionSpec as P


HD = 128
LANES = 128
SHARES = (1, 2)
BLOCK = 256
LOG2E = float(np.log2(np.e))


def params(mib):
    return pltpu.CompilerParams(vmem_limit_bytes=mib * 1024 * 1024)


def in_hbm(x):
    return pltpu.with_memory_space_constraint(x, pltpu.HBM)


def softmax_rows(query, keys, values, masks, scale):
    scores = []
    for key, mask in zip(keys, masks):
        s = lax.dot_general(query, key, (((1,), (1,)), ((), ())), preferred_element_type=jnp.float32)
        scores.append(s if mask is None else jnp.where(mask, s, -jnp.inf))
    largest = functools.reduce(jnp.maximum, [jnp.max(s, axis=1, keepdims=True) for s in scores])
    total = None
    for s, value in zip(scores, values):
        weights = jnp.exp2((s - largest) * (scale * LOG2E)).astype(jnp.bfloat16)
        ones = jnp.ones((value.shape[0], LANES), jnp.bfloat16)
        part = jnp.dot(weights, jnp.concatenate([value, ones], axis=1), preferred_element_type=jnp.float32)
        total = part if total is None else total + part
    head = value.shape[1]
    sums = total[:, head : head + LANES]
    return total[:, :head] / sums, largest * (scale * LOG2E) + jnp.log2(sums[:, :1])


def column_copies(place_ref, offsets, w_hbm, w_ref, sems, first):
    chunk = w_ref.shape[2] // len(offsets)
    copies = []
    for i, offset in enumerate(offsets):
        start = pl.multiple_of(jnp.bitwise_xor(place_ref[1], offset) * chunk, chunk)
        src, dst = w_hbm.at[:, :, pl.ds(start, chunk)], w_ref.at[:, :, pl.ds(i * chunk, chunk)]
        copies.append(pltpu.make_async_copy(src, dst, sems.at[first + i]))
    return copies


def own_kernel(offsets, loads, place_ref, kinds_ref, q_hbm, k_hbm, v_hbm, w_hbm, *refs):
    others = len(offsets) - 1
    k_refs, v_refs = refs[:others], refs[others : 2 * others]
    out_ref, lse_ref, k_ref, v_ref, columns_ref, w_ref, q_ref, sems = refs[2 * others :]
    pairs = [(q_hbm, q_ref), (k_hbm, k_ref), (v_hbm, v_ref)]
    copies = [pltpu.make_async_copy(src, dst, sems.at[i]) for i, (src, dst) in enumerate(pairs)]
    later = column_copies(place_ref, loads, w_hbm, w_ref, sems, len(pairs))
    for copy in copies + later:
        copy.start()
    me = place_ref[0]
    rows = q_ref.shape[0]
    columns_ref[...] = jnp.broadcast_to(kinds_ref[...].astype(jnp.float32), (LANES, rows)).T
    for copy in copies:
        copy.wait()
    below = lax.broadcasted_iota(jnp.int32, (rows, rows), 0) >= lax.broadcasted_iota(jnp.int32, (rows, rows), 1)
    masks = [below if o == 0 else lax.broadcast(jnp.bitwise_xor(me, o), (rows, rows)) < me for o in offsets]
    for h in range(q_ref.shape[1] // HD):
        at = slice(h * HD, (h + 1) * HD)
        keys = [k[:, at] for k in (k_ref, *k_refs)]
        vals = [v[:, at] for v in (v_ref, *v_refs)]
        result, lse = softmax_rows(q_ref[:, at], keys, vals, masks, HD**-0.5)
        out_ref[:, at] = result.astype(out_ref.dtype)
        lse_ref[:, h : h + 1] = lse
    for copy in later:
        copy.wait()


def put_lse(found, h, shipped, lse):
    lanes = lax.broadcasted_iota(jnp.int32, found.shape, 1)
    return jnp.where(lanes % shipped == h, lse, found)


def lse_terms(found, shipped):
    lanes = lax.broadcasted_iota(jnp.int32, found.shape, 1)
    high = found.astype(jnp.bfloat16).astype(jnp.float32)
    middle = (found - high).astype(jnp.bfloat16).astype(jnp.float32)
    low = found - high - middle
    return jnp.where(lanes < shipped, high, jnp.where(lanes < 2 * shipped, middle, low))


def lse_rows(shipped):
    return -(-3 * shipped // 16) * 16


def cross_kernel(count, half, skip, loads, place_ref, q_ref, *refs):
    k_refs, v_refs = refs[:count], refs[count : 2 * count]
    later = []
    if loads:
        w_hbm, out_ref, w_ref, sems = refs[2 * count :]
        later = column_copies(place_ref, loads, w_hbm, w_ref, sems, 0)
    else:
        (out_ref,) = refs[2 * count :]
    for copy in later:
        copy.start()
    rows, width = q_ref.shape
    shipped = width // HD

    @pl.when(place_ref[0] < half)
    def _():
        found = jnp.zeros((rows, LANES), jnp.float32)
        for h in range(width // HD):
            at, there = slice(h * HD, (h + 1) * HD), slice(skip + h * HD, skip + (h + 1) * HD)
            result, lse = softmax_rows(
                q_ref[:, at], [k[:, there] for k in k_refs], [v[:, there] for v in v_refs], [None] * count, HD**-0.5
            )
            out_ref[:rows, at] = result.astype(out_ref.dtype)
            found = put_lse(found, h, shipped, lse)
        extra = out_ref.shape[0] - rows
        out_ref[rows:, :rows] = lse_terms(found, shipped).T[:extra].astype(out_ref.dtype)

    for copy in later:
        copy.wait()


def mix(own, own_lse, far, far_lse, out_dtype):
    mine = 1.0 / (1.0 + jnp.exp2(far_lse - own_lse))
    return (own.astype(jnp.float32) * mine + far.astype(jnp.float32) * (1.0 - mine)).astype(out_dtype)


def far_kernel(count, half, place_ref, q_hbm, own_ref, lse_ref, *refs):
    k_refs, v_refs = refs[:count], refs[count : 2 * count]
    out_ref, q_ref, sem = refs[2 * count :]
    width = out_ref.shape[1]
    copy = pltpu.make_async_copy(q_hbm.at[:, :width], q_ref, sem)
    copy.start()
    copy.wait()

    @pl.when(place_ref[0] < half)
    def _():
        out_ref[...] = own_ref[:, :width]

    @pl.when(place_ref[0] >= half)
    def _():
        for h in range(width // HD):
            at = slice(h * HD, (h + 1) * HD)
            result, lse = softmax_rows(
                q_ref[:, at], [k[:, at] for k in k_refs], [v[:, at] for v in v_refs], [None] * count, HD**-0.5
            )
            out_ref[:, at] = mix(own_ref[:, at], lse_ref[:, h : h + 1], result, lse, out_ref.dtype)


def project(rows, image, first, w_ref, out_ref):
    chunk = out_ref.shape[1]
    block = min(chunk, BLOCK)
    nothing = jnp.zeros_like(rows)
    text_rows, image_rows = jnp.where(image, nothing, rows), jnp.where(image, rows, nothing)
    for b in range(0, chunk, block):
        at = slice(first + b, first + b + block)
        total = jnp.dot(text_rows, w_ref[0, :, at], preferred_element_type=jnp.float32)
        total += jnp.dot(image_rows, w_ref[1, :, at], preferred_element_type=jnp.float32)
        out_ref[:, b : b + block] = total.astype(out_ref.dtype)


def merge_kernel(half, lo, first, place_ref, own_ref, lse_ref, near_ref, back_ref, kinds_ref, w_ref, att_ref, out_ref):
    count, _ = att_ref.shape
    rows = slice(lo, lo + count)
    skip, shipped = near_ref.shape[1], back_ref.shape[1] // HD
    att_ref[:, :skip] = near_ref[rows, :]

    @pl.when(place_ref[0] < half)
    def _():
        att_ref[:, skip:] = own_ref[rows, skip:]

    @pl.when(place_ref[0] >= half)
    def _():
        terms = back_ref[own_ref.shape[0] :, rows].astype(jnp.float32)
        terms = jnp.concatenate([terms, jnp.zeros((LANES - terms.shape[0], count), jnp.float32)], axis=0).T
        for h in range(shipped):
            at, there = slice(h * HD, (h + 1) * HD), slice(skip + h * HD, skip + (h + 1) * HD)
            far_lse = sum(terms[:, c : c + 1] for c in (h, shipped + h, 2 * shipped + h))
            own_h = skip // HD + h
            att_ref[:, there] = mix(
                own_ref[rows, there], lse_ref[rows, own_h : own_h + 1], back_ref[rows, at], far_lse, att_ref.dtype
            )

    project(att_ref[...], kinds_ref[rows, :1] == 1, first, w_ref, out_ref)


def project_kernel(lo, first, kinds_ref, w_ref, *refs):
    att_refs, out_ref = refs[:-1], refs[-1]
    rows = jnp.concatenate([x[...] for x in att_refs], axis=0)
    project(rows, kinds_ref[lo : lo + rows.shape[0], :1] == 1, first, w_ref, out_ref)


def on_device(queries, key_rows, values, modality, out_weight):
    seq_count = lax.axis_size("seq")
    tp_count = lax.axis_size("tp")
    half = seq_count // 2
    place = jnp.stack([lax.axis_index("seq"), lax.axis_index("tp")]).astype(jnp.int32)
    rows, width = queries.shape
    chunk = out_weight.shape[2] // tp_count
    vmem = pl.BlockSpec(memory_space=pltpu.VMEM)
    smem = pl.BlockSpec(memory_space=pltpu.SMEM)
    hbm = pl.BlockSpec(memory_space=pltpu.HBM)
    edges = [0, *(rows * share // SHARES[-1] for share in SHARES)]
    parts = list(zip(edges[:-1], edges[1:]))

    def xor(count, bit):
        return [(i, i ^ bit) for i in range(count)]

    order = sorted(range(tp_count), reverse=True)
    early_loads, late_loads = order[: tp_count // 2], order[tp_count // 2 :]

    def columns_shape(loads):
        return jax.ShapeDtypeStruct((out_weight.shape[0], width, chunk * len(loads)), out_weight.dtype)

    offsets, keys, vals = [0], [key_rows], [values]
    bit = half // 2
    while bit:
        keys = keys + [lax.ppermute(x, "seq", xor(seq_count, bit)) for x in keys]
        vals = vals + [lax.ppermute(x, "seq", xor(seq_count, bit)) for x in vals]
        offsets = offsets + [o ^ bit for o in offsets]
        bit //= 2
    count = len(offsets)

    heads = width // HD
    shipped = heads // 2
    skip = (heads - shipped) * HD
    up = [(i, i + half) for i in range(half)]
    met = lax.ppermute(
        jnp.where(place[0] >= half, queries[:, skip:], key_rows[:, : width - skip]), "seq", xor(seq_count, half)
    )
    far_keys = [met]
    far_vals = [lax.ppermute(values[:, :skip], "seq", up)]
    bit = half // 2
    while bit:
        far_keys = far_keys + [lax.ppermute(x, "seq", xor(seq_count, bit)) for x in far_keys]
        far_vals = far_vals + [lax.ppermute(x, "seq", xor(seq_count, bit)) for x in far_vals]
        bit //= 2

    own, own_lse, keys[0], vals[0], kinds, early = pl.pallas_call(
        functools.partial(own_kernel, tuple(offsets), tuple(early_loads)),
        out_shape=(
            jax.ShapeDtypeStruct((rows, width), jnp.bfloat16),
            jax.ShapeDtypeStruct((rows, LANES), jnp.float32),
            jax.ShapeDtypeStruct(key_rows.shape, key_rows.dtype),
            jax.ShapeDtypeStruct(values.shape, values.dtype),
            jax.ShapeDtypeStruct((rows, LANES), jnp.float32),
            columns_shape(early_loads),
        ),
        in_specs=[smem, vmem] + [hbm] * 4 + [vmem] * (2 * count - 2),
        out_specs=(vmem,) * 6,
        scratch_shapes=[
            pltpu.VMEM(queries.shape, queries.dtype),
            pltpu.SemaphoreType.DMA((3 + len(early_loads),)),
        ],
        compiler_params=params(8),
        name="own",
    )(place, modality.reshape(1, rows), *(in_hbm(x) for x in (queries, key_rows, values, out_weight)), *keys[1:], *vals[1:])

    loads = tuple(late_loads)
    found, late = pl.pallas_call(
        functools.partial(cross_kernel, count, half, skip, loads),
        out_shape=(jax.ShapeDtypeStruct((rows + lse_rows(shipped), width - skip), jnp.bfloat16), columns_shape(loads)),
        in_specs=[smem] + [vmem] * (1 + 2 * count) + [hbm],
        out_specs=(vmem, vmem),
        scratch_shapes=[pltpu.SemaphoreType.DMA((len(loads),))],
        compiler_params=params(8),
        name="cross",
    )(place, met, *keys, *vals, in_hbm(out_weight))
    back = lax.ppermute(found, "seq", up)
    near = pl.pallas_call(
        functools.partial(far_kernel, count, half),
        out_shape=jax.ShapeDtypeStruct((rows, skip), jnp.bfloat16),
        in_specs=[smem, hbm] + [vmem] * (2 + 2 * count),
        out_specs=vmem,
        scratch_shapes=[pltpu.VMEM((rows, skip), jnp.bfloat16), pltpu.SemaphoreType.DMA],
        compiler_params=params(8),
        name="far",
    )(place, in_hbm(queries), own, own_lse, *far_keys, *far_vals)

    def columns_of(offset):
        if offset in early_loads:
            return early, early_loads.index(offset) * chunk
        return late, late_loads.index(offset) * chunk

    def merged(p, offset):
        weight, first = columns_of(offset)
        lo, hi = parts[p]
        return pl.pallas_call(
            functools.partial(merge_kernel, half, lo, first),
            out_shape=(
                jax.ShapeDtypeStruct((hi - lo, width), jnp.bfloat16),
                jax.ShapeDtypeStruct((hi - lo, chunk), jnp.bfloat16),
            ),
            in_specs=[smem] + [vmem] * 6,
            out_specs=(vmem, vmem),
            compiler_params=params(8),
            name="merge",
        )(place, own, own_lse, near, back, kinds, weight)

    def projected(lo, attended, offset):
        weight, first = columns_of(offset)
        return pl.pallas_call(
            functools.partial(project_kernel, lo, first),
            out_shape=jax.ShapeDtypeStruct((sum(x.shape[0] for x in attended), chunk), jnp.bfloat16),
            in_specs=[vmem] * (2 + len(attended)),
            out_specs=vmem,
            compiler_params=params(8),
            name="project",
        )(kinds, weight, *attended)

    def add(*terms):
        return sum(x.astype(jnp.float32) for x in terms)

    attended, sums = [], []
    for p in range(len(parts)):
        here, first = merged(p, tp_count - 1)
        attended.append(here)
        have = {tp_count - 1: first}
        for offset in range(2, tp_count - 1):
            have[offset] = projected(parts[p][0], [here], offset)
        bit, arrivals = 1, []
        while bit < tp_count:
            keep = dict(have)
            for offset in sorted(have, reverse=True):
                if offset & bit:
                    arrived = lax.ppermute(keep.pop(offset), "tp", xor(tp_count, bit))
                    if offset == bit:
                        arrivals.append(arrived)
                    else:
                        keep[offset ^ bit] = add(have[offset ^ bit], arrived).astype(jnp.bfloat16)
            have = keep
            bit *= 2
        sums.append(arrivals)
    beside = projected(0, attended, 1)
    beside = lax.ppermute(beside, "tp", xor(tp_count, 1))
    total = projected(0, attended, 0)
    total = add(total, beside)
    for arrivals in zip(*sums):
        total = add(total, jnp.concatenate(arrivals, axis=0))
    return total.astype(jnp.bfloat16)


def solution(mesh):
    in_specs = (
        P(("dp", "seq"), "tp"),
        P(("dp", "seq"), "tp"),
        P(("dp", "seq"), "tp"),
        P(("dp", "seq")),
        P(None, "tp", None),
    )
    out_specs = P(("dp", "seq"), "tp")

    return jax.shard_map(on_device, mesh=mesh, in_specs=in_specs, out_specs=out_specs, check_vma=False)
```

```python
import functools

import jax
import jax.numpy as jnp
import numpy as np
from jax import lax
from jax.experimental import pallas as pl
from jax.experimental.pallas import tpu as pltpu
from jax.sharding import PartitionSpec as P


HD = 128
LANES = 128
SHARES = (1, 2)
BLOCK = 256
PIECES = 4
LOG2E = float(np.log2(np.e))


def params(mib):
    return pltpu.CompilerParams(vmem_limit_bytes=mib * 1024 * 1024)


def in_hbm(x):
    return pltpu.with_memory_space_constraint(x, pltpu.HBM)


def softmax_rows(query, keys, values, masks, scale):
    scores = []
    for key, mask in zip(keys, masks):
        s = lax.dot_general(query, key, (((1,), (1,)), ((), ())), preferred_element_type=jnp.float32)
        scores.append(s if mask is None else jnp.where(mask, s, -jnp.inf))
    largest = functools.reduce(jnp.maximum, [jnp.max(s, axis=1, keepdims=True) for s in scores])
    total = None
    for s, value in zip(scores, values):
        weights = jnp.exp2((s - largest) * (scale * LOG2E)).astype(jnp.bfloat16)
        ones = jnp.ones((value.shape[0], LANES), jnp.bfloat16)
        part = jnp.dot(weights, jnp.concatenate([value, ones], axis=1), preferred_element_type=jnp.float32)
        total = part if total is None else total + part
    head = value.shape[1]
    sums = total[:, head : head + LANES]
    return total[:, :head] / sums, largest * (scale * LOG2E) + jnp.log2(sums[:, :1])


def column_copies(place_ref, offsets, w_hbm, w_ref, sems, first):
    kinds, depth, width = w_ref.shape
    chunk = width // len(offsets)
    piece = depth // PIECES
    copies = []
    for i, offset in enumerate(offsets):
        start = pl.multiple_of(jnp.bitwise_xor(place_ref[1], offset) * chunk, chunk)
        for kind in range(kinds):
            for rows in (pl.ds(r * piece, piece) for r in range(PIECES)):
                src = w_hbm.at[kind, rows, pl.ds(start, chunk)]
                dst = w_ref.at[kind, rows, pl.ds(i * chunk, chunk)]
                copies.append(pltpu.make_async_copy(src, dst, sems.at[first + len(copies)]))
    return copies


def own_kernel(offsets, loads, place_ref, kinds_hbm, q_hbm, k_hbm, v_hbm, w_hbm, *refs):
    others = len(offsets) - 1
    k_refs, v_refs = refs[:others], refs[others : 2 * others]
    out_ref, lse_ref, q_ref, k_ref, v_ref, columns_ref, w_ref, kinds_ref, sems = refs[2 * others :]
    pairs = [(kinds_hbm, kinds_ref), (v_hbm, v_ref), (q_hbm, q_ref), (k_hbm, k_ref)]
    copies = [pltpu.make_async_copy(src, dst, sems.at[i]) for i, (src, dst) in enumerate(pairs)]
    later = column_copies(place_ref, loads, w_hbm, w_ref, sems, len(pairs))
    for copy in copies + later:
        copy.start()
    me = place_ref[0]
    rows = q_ref.shape[0]
    for copy in copies:
        copy.wait()
    lse_ref[...] = jnp.zeros_like(lse_ref)
    columns_ref[...] = jnp.broadcast_to(kinds_ref[...].astype(jnp.float32), (LANES, rows)).T
    below = lax.broadcasted_iota(jnp.int32, (rows, rows), 0) >= lax.broadcasted_iota(jnp.int32, (rows, rows), 1)
    masks = [below if o == 0 else lax.broadcast(jnp.bitwise_xor(me, o), (rows, rows)) < me for o in offsets]
    for h in range(q_ref.shape[1] // HD):
        at = slice(h * HD, (h + 1) * HD)
        keys = [k[:, at] for k in (k_ref, *k_refs)]
        vals = [v[:, at] for v in (v_ref, *v_refs)]
        result, lse = softmax_rows(q_ref[:, at], keys, vals, masks, HD**-0.5)
        out_ref[:, at] = result.astype(out_ref.dtype)
        lse_ref[:, h : h + 1] = lse
    for copy in later:
        copy.wait()


def put_lse(found, h, shipped, lse):
    lanes = lax.broadcasted_iota(jnp.int32, found.shape, 1)
    return jnp.where(lanes % shipped == h, lse, found)


def lse_terms(found, shipped):
    lanes = lax.broadcasted_iota(jnp.int32, found.shape, 1)
    high = found.astype(jnp.bfloat16).astype(jnp.float32)
    middle = (found - high).astype(jnp.bfloat16).astype(jnp.float32)
    low = found - high - middle
    return jnp.where(lanes < shipped, high, jnp.where(lanes < 2 * shipped, middle, low))


def lse_rows(shipped):
    return -(-3 * shipped // 16) * 16


def cross_kernel(count, half, skip, place_ref, q_ref, *refs):
    k_refs, v_refs = refs[:count], refs[count : 2 * count]
    (out_ref,) = refs[2 * count :]
    rows, width = q_ref.shape
    shipped = width // HD

    @pl.when(place_ref[0] < half)
    def _():
        found = jnp.zeros((rows, LANES), jnp.float32)
        for h in range(width // HD):
            at, there = slice(h * HD, (h + 1) * HD), slice(skip + h * HD, skip + (h + 1) * HD)
            result, lse = softmax_rows(
                q_ref[:, at], [k[:, there] for k in k_refs], [v[:, there] for v in v_refs], [None] * count, HD**-0.5
            )
            out_ref[:rows, at] = result.astype(out_ref.dtype)
            found = put_lse(found, h, shipped, lse)
        extra = out_ref.shape[0] - rows
        out_ref[rows:, :rows] = lse_terms(found, shipped).T[:extra].astype(out_ref.dtype)


def mix(own, far, share, out_dtype):
    return (own.astype(jnp.float32) * share + far.astype(jnp.float32) * (1.0 - share)).astype(out_dtype)


def load_kernel(loads, place_ref, w_hbm, w_ref, sems):
    copies = column_copies(place_ref, loads, w_hbm, w_ref, sems, 0)
    for copy in copies:
        copy.start()
    for copy in copies:
        copy.wait()


def far_kernel(count, half, place_ref, q_ref, own_ref, lse_ref, *refs):
    k_refs, v_refs = refs[:count], refs[count : 2 * count]
    (out_ref,) = refs[2 * count :]
    width = out_ref.shape[1]

    @pl.when(place_ref[0] < half)
    def _():
        out_ref[...] = own_ref[:, :width]

    @pl.when(place_ref[0] >= half)
    def _():
        for h in range(width // HD):
            at = slice(h * HD, (h + 1) * HD)
            result, lse = softmax_rows(
                q_ref[:, at], [k[:, at] for k in k_refs], [v[:, at] for v in v_refs], [None] * count, HD**-0.5
            )
            share = 1.0 / (1.0 + jnp.exp2(lse - lse_ref[:, h : h + 1]))
            out_ref[:, at] = mix(own_ref[:, at], result, share, out_ref.dtype)


def project(rows, image, first, w_ref, out_ref):
    chunk = out_ref.shape[1]
    block = min(chunk, BLOCK)
    nothing = jnp.zeros_like(rows)
    text_rows, image_rows = jnp.where(image, nothing, rows), jnp.where(image, rows, nothing)
    for b in range(0, chunk, block):
        at = slice(first + b, first + b + block)
        total = jnp.dot(text_rows, w_ref[0, :, at], preferred_element_type=jnp.float32)
        total += jnp.dot(image_rows, w_ref[1, :, at], preferred_element_type=jnp.float32)
        out_ref[:, b : b + block] = total.astype(out_ref.dtype)


def merge_kernel(half, lo, first, place_ref, own_ref, lse_ref, near_ref, back_ref, kinds_ref, w_ref, att_ref, out_ref):
    count, _ = att_ref.shape
    rows = slice(lo, lo + count)
    skip, shipped = near_ref.shape[1], back_ref.shape[1] // HD
    att_ref[:, :skip] = near_ref[rows, :]

    @pl.when(place_ref[0] < half)
    def _():
        att_ref[:, skip:] = own_ref[rows, skip:]

    @pl.when(place_ref[0] >= half)
    def _():
        terms = back_ref[own_ref.shape[0] :, rows].astype(jnp.float32)
        far_lse = sum(terms[i * shipped : (i + 1) * shipped] for i in range(3))
        before = skip // HD
        far_lse = jnp.concatenate(
            [
                jnp.zeros((before, count), jnp.float32),
                far_lse,
                jnp.zeros((LANES - before - shipped, count), jnp.float32),
            ],
            axis=0,
        ).T
        mine = 1.0 / (1.0 + jnp.exp2(far_lse - lse_ref[rows, :]))
        for h in range(shipped):
            at, there = slice(h * HD, (h + 1) * HD), slice(skip + h * HD, skip + (h + 1) * HD)
            share = mine[:, before + h : before + h + 1]
            att_ref[:, there] = mix(own_ref[rows, there], back_ref[rows, at], share, att_ref.dtype)

    project(att_ref[...], kinds_ref[rows, :1] == 1, first, w_ref, out_ref)


def stream_kernel(offset, place_ref, w_hbm, kinds_ref, *refs):
    *att_refs, out_ref, w_ref, sems = refs
    copies = column_copies(place_ref, (offset,), w_hbm, w_ref, sems, 0)
    for copy in copies:
        copy.start()
    for copy in copies:
        copy.wait()
    project_kernel(0, 0, kinds_ref, w_ref, *att_refs, out_ref)


def project_kernel(lo, first, kinds_ref, w_ref, *refs):
    att_refs, out_ref = refs[:-1], refs[-1]
    rows = jnp.concatenate([x[...] for x in att_refs], axis=0)
    project(rows, kinds_ref[lo : lo + rows.shape[0], :1] == 1, first, w_ref, out_ref)


def on_device(queries, key_rows, values, modality, out_weight):
    seq_count = lax.axis_size("seq")
    tp_count = lax.axis_size("tp")
    half = seq_count // 2
    place = jnp.stack([lax.axis_index("seq"), lax.axis_index("tp")]).astype(jnp.int32)
    rows, width = queries.shape
    chunk = out_weight.shape[2] // tp_count
    vmem = pl.BlockSpec(memory_space=pltpu.VMEM)
    smem = pl.BlockSpec(memory_space=pltpu.SMEM)
    hbm = pl.BlockSpec(memory_space=pltpu.HBM)
    edges = [0, *(rows * share // SHARES[-1] for share in SHARES)]
    parts = list(zip(edges[:-1], edges[1:]))

    def xor(count, bit):
        return [(i, i ^ bit) for i in range(count)]

    order = sorted(range(tp_count), reverse=True)
    loads = [tuple(order[:1]), tuple(order[1:-1])]
    columns = {}
    pieces = PIECES * out_weight.shape[0]

    def columns_shape(loads):
        return jax.ShapeDtypeStruct((out_weight.shape[0], width, chunk * len(loads)), out_weight.dtype)

    heads = width // HD
    shipped = heads // 2
    skip = (heads - shipped) * HD
    up = [(i, i + half) for i in range(half)]
    met = lax.ppermute(
        jnp.where(place[0] >= half, queries[:, skip:], key_rows[:, : width - skip]), "seq", xor(seq_count, half)
    )
    offsets, keys, vals = [0], [key_rows], [values]
    bit = half // 2
    while bit:
        keys = keys + [lax.ppermute(x, "seq", xor(seq_count, bit)) for x in keys]
        vals = vals + [lax.ppermute(x, "seq", xor(seq_count, bit)) for x in vals]
        offsets = offsets + [o ^ bit for o in offsets]
        bit //= 2
    count = len(offsets)

    own, own_lse, own_queries, keys[0], vals[0], kinds, columns[loads[0]] = pl.pallas_call(
        functools.partial(own_kernel, tuple(offsets), loads[0]),
        out_shape=(
            jax.ShapeDtypeStruct((rows, width), jnp.bfloat16),
            jax.ShapeDtypeStruct((rows, LANES), jnp.float32),
            jax.ShapeDtypeStruct(queries.shape, queries.dtype),
            jax.ShapeDtypeStruct(key_rows.shape, key_rows.dtype),
            jax.ShapeDtypeStruct(values.shape, values.dtype),
            jax.ShapeDtypeStruct((rows, LANES), jnp.float32),
            columns_shape(loads[0]),
        ),
        in_specs=[smem] + [hbm] * 5 + [vmem] * (2 * count - 2),
        out_specs=(vmem,) * 7,
        scratch_shapes=[pltpu.VMEM((1, rows), modality.dtype), pltpu.SemaphoreType.DMA((4 + pieces * len(loads[0]),))],
        compiler_params=params(8),
        name="own",
    )(
        place,
        *(in_hbm(x) for x in (modality.reshape(1, rows), queries, key_rows, values, out_weight)),
        *keys[1:],
        *vals[1:],
    )
    far_keys = [met]
    far_vals = [lax.ppermute(values[:, :skip], "seq", up)]
    bit = half // 2
    while bit:
        far_keys = far_keys + [lax.ppermute(x, "seq", xor(seq_count, bit)) for x in far_keys]
        far_vals = far_vals + [lax.ppermute(x, "seq", xor(seq_count, bit)) for x in far_vals]
        bit //= 2


    found = pl.pallas_call(
        functools.partial(cross_kernel, count, half, skip),
        out_shape=jax.ShapeDtypeStruct((rows + lse_rows(shipped), width - skip), jnp.bfloat16),
        in_specs=[smem] + [vmem] * (1 + 2 * count),
        out_specs=vmem,
        compiler_params=params(8),
        name="cross",
    )(place, met, *keys, *vals)
    back = lax.ppermute(found, "seq", up)
    near = pl.pallas_call(
        functools.partial(far_kernel, count, half),
        out_shape=jax.ShapeDtypeStruct((rows, skip), jnp.bfloat16),
        in_specs=[smem] + [vmem] * (3 + 2 * count),
        out_specs=vmem,
        compiler_params=params(8),
        name="far",
    )(place, own_queries, own, own_lse, *far_keys, *far_vals)
    columns[loads[1]] = pl.pallas_call(
        functools.partial(load_kernel, loads[1]),
        out_shape=columns_shape(loads[1]),
        in_specs=[smem, hbm],
        out_specs=vmem,
        scratch_shapes=[pltpu.SemaphoreType.DMA((pieces * len(loads[1]),))],
        compiler_params=params(8),
        name="load",
    )(place, in_hbm(out_weight))

    def columns_of(offset):
        (held,) = (x for x in loads if offset in x)
        return columns[held], held.index(offset) * chunk

    def merged(p, offset):
        weight, first = columns_of(offset)
        lo, hi = parts[p]
        return pl.pallas_call(
            functools.partial(merge_kernel, half, lo, first),
            out_shape=(
                jax.ShapeDtypeStruct((hi - lo, width), jnp.bfloat16),
                jax.ShapeDtypeStruct((hi - lo, chunk), jnp.bfloat16),
            ),
            in_specs=[smem] + [vmem] * 6,
            out_specs=(vmem, vmem),
            compiler_params=params(8),
            name="merge",
        )(place, own, own_lse, near, back, kinds, weight)

    def streamed(attended, offset):
        return pl.pallas_call(
            functools.partial(stream_kernel, offset),
            out_shape=jax.ShapeDtypeStruct((rows, chunk), jnp.bfloat16),
            in_specs=[smem, hbm] + [vmem] * (1 + len(attended)),
            out_specs=vmem,
            scratch_shapes=[
                pltpu.VMEM((out_weight.shape[0], width, chunk), out_weight.dtype),
                pltpu.SemaphoreType.DMA((pieces,)),
            ],
            compiler_params=params(12),
            name="stream",
        )(place, in_hbm(out_weight), kinds, *attended)

    def projected(lo, attended, offset):
        weight, first = columns_of(offset)
        return pl.pallas_call(
            functools.partial(project_kernel, lo, first),
            out_shape=jax.ShapeDtypeStruct((sum(x.shape[0] for x in attended), chunk), jnp.bfloat16),
            in_specs=[vmem] * (2 + len(attended)),
            out_specs=vmem,
            compiler_params=params(8),
            name="project",
        )(kinds, weight, *attended)

    def add(*terms):
        return sum(x.astype(jnp.float32) for x in terms)

    attended, sums = [], []
    for p in range(len(parts)):
        here, first = merged(p, tp_count - 1)
        attended.append(here)
        have = {tp_count - 1: first}
        for offset in range(2, tp_count - 1):
            have[offset] = projected(parts[p][0], [here], offset)
        bit, arrivals = 1, []
        while bit < tp_count:
            keep = dict(have)
            for offset in sorted(have, reverse=True):
                if offset & bit:
                    arrived = lax.ppermute(keep.pop(offset), "tp", xor(tp_count, bit))
                    if offset == bit:
                        arrivals.append(arrived)
                    else:
                        keep[offset ^ bit] = add(have[offset ^ bit], arrived).astype(jnp.bfloat16)
            have = keep
            bit *= 2
        sums.append(arrivals)
    beside = projected(0, attended, 1)
    beside = lax.ppermute(beside, "tp", xor(tp_count, 1))
    total = streamed(attended, 0)
    total = add(total, beside)
    for arrivals in zip(*sums):
        total = add(total, jnp.concatenate(arrivals, axis=0))
    return total.astype(jnp.bfloat16)


def solution(mesh):
    in_specs = (
        P(("dp", "seq"), "tp"),
        P(("dp", "seq"), "tp"),
        P(("dp", "seq"), "tp"),
        P(("dp", "seq")),
        P(None, "tp", None),
    )
    out_specs = P(("dp", "seq"), "tp")

    return jax.shard_map(on_device, mesh=mesh, in_specs=in_specs, out_specs=out_specs, check_vma=False)
```

```python
import functools

import jax
import jax.numpy as jnp
import numpy as np
from jax import lax
from jax.experimental import pallas as pl
from jax.experimental.pallas import tpu as pltpu
from jax.sharding import PartitionSpec as P


HD = 128
LANES = 128
SHARES = (1, 2)
BLOCK = 256
PIECES = 4
LOG2E = float(np.log2(np.e))


def params(mib):
    return pltpu.CompilerParams(vmem_limit_bytes=mib * 1024 * 1024)


def in_hbm(x):
    return pltpu.with_memory_space_constraint(x, pltpu.HBM)


def softmax_rows(query, keys, values, masks, scale):
    scores = []
    for key, mask in zip(keys, masks):
        s = lax.dot_general(query, key, (((1,), (1,)), ((), ())), preferred_element_type=jnp.float32)
        scores.append(s if mask is None else jnp.where(mask, s, -jnp.inf))
    largest = functools.reduce(jnp.maximum, [jnp.max(s, axis=1, keepdims=True) for s in scores])
    total = None
    for s, value in zip(scores, values):
        weights = jnp.exp2((s - largest) * (scale * LOG2E)).astype(jnp.bfloat16)
        ones = jnp.ones((value.shape[0], LANES), jnp.bfloat16)
        part = jnp.dot(weights, jnp.concatenate([value, ones], axis=1), preferred_element_type=jnp.float32)
        total = part if total is None else total + part
    head = value.shape[1]
    sums = total[:, head : head + LANES]
    return total[:, :head] / sums, largest * (scale * LOG2E) + jnp.log2(sums[:, :1])


def column_copies(place_ref, offsets, w_hbm, w_ref, sems, first):
    kinds, depth, width = w_ref.shape
    chunk = width // len(offsets)
    piece = depth // PIECES
    copies = []
    for i, offset in enumerate(offsets):
        start = pl.multiple_of(jnp.bitwise_xor(place_ref[1], offset) * chunk, chunk)
        for kind in range(kinds):
            for rows in (pl.ds(r * piece, piece) for r in range(PIECES)):
                src = w_hbm.at[kind, rows, pl.ds(start, chunk)]
                dst = w_ref.at[kind, rows, pl.ds(i * chunk, chunk)]
                copies.append(pltpu.make_async_copy(src, dst, sems.at[first + len(copies)]))
    return copies


def own_kernel(offsets, loads, place_ref, kinds_hbm, q_hbm, k_hbm, v_hbm, w_hbm, *refs):
    others = len(offsets) - 1
    k_refs, v_refs = refs[:others], refs[others : 2 * others]
    out_ref, lse_ref, q_ref, k_ref, v_ref, columns_ref, w_ref, kinds_ref, sems = refs[2 * others :]
    pairs = [(kinds_hbm, kinds_ref), (v_hbm, v_ref), (q_hbm, q_ref), (k_hbm, k_ref)]
    copies = [pltpu.make_async_copy(src, dst, sems.at[i]) for i, (src, dst) in enumerate(pairs)]
    later = column_copies(place_ref, loads, w_hbm, w_ref, sems, len(pairs))
    for copy in copies + later:
        copy.start()
    me = place_ref[0]
    rows = q_ref.shape[0]
    for copy in copies:
        copy.wait()
    lse_ref[...] = jnp.zeros_like(lse_ref)
    columns_ref[...] = jnp.broadcast_to(kinds_ref[...].astype(jnp.float32), (LANES, rows)).T
    below = lax.broadcasted_iota(jnp.int32, (rows, rows), 0) >= lax.broadcasted_iota(jnp.int32, (rows, rows), 1)
    masks = [below if o == 0 else lax.broadcast(jnp.bitwise_xor(me, o), (rows, rows)) < me for o in offsets]
    for h in range(q_ref.shape[1] // HD):
        at = slice(h * HD, (h + 1) * HD)
        keys = [k[:, at] for k in (k_ref, *k_refs)]
        vals = [v[:, at] for v in (v_ref, *v_refs)]
        result, lse = softmax_rows(q_ref[:, at], keys, vals, masks, HD**-0.5)
        out_ref[:, at] = result.astype(out_ref.dtype)
        lse_ref[:, h : h + 1] = lse
    for copy in later:
        copy.wait()


def put_lse(found, h, shipped, lse):
    lanes = lax.broadcasted_iota(jnp.int32, found.shape, 1)
    return jnp.where(lanes % shipped == h, lse, found)


def lse_terms(found, shipped):
    lanes = lax.broadcasted_iota(jnp.int32, found.shape, 1)
    high = found.astype(jnp.bfloat16).astype(jnp.float32)
    middle = (found - high).astype(jnp.bfloat16).astype(jnp.float32)
    low = found - high - middle
    return jnp.where(lanes < shipped, high, jnp.where(lanes < 2 * shipped, middle, low))


def lse_rows(shipped):
    return -(-3 * shipped // 16) * 16


def cross_kernel(count, half, skip, lo, place_ref, q_ref, *refs):
    k_refs, v_refs = refs[:count], refs[count : 2 * count]
    (out_ref,) = refs[2 * count :]
    width = q_ref.shape[1]
    shipped = width // HD
    extra = lse_rows(shipped)
    rows = out_ref.shape[0] - extra

    @pl.when(place_ref[0] < half)
    def _():
        found = jnp.zeros((rows, LANES), jnp.float32)
        for h in range(width // HD):
            at, there = slice(h * HD, (h + 1) * HD), slice(skip + h * HD, skip + (h + 1) * HD)
            query = q_ref[lo : lo + rows, at]
            result, lse = softmax_rows(
                query, [k[:, there] for k in k_refs], [v[:, there] for v in v_refs], [None] * count, HD**-0.5
            )
            out_ref[:rows, at] = result.astype(out_ref.dtype)
            found = put_lse(found, h, shipped, lse)
        out_ref[rows:, :rows] = lse_terms(found, shipped).T[:extra].astype(out_ref.dtype)


def mix(own, far, share, out_dtype):
    return (own.astype(jnp.float32) * share + far.astype(jnp.float32) * (1.0 - share)).astype(out_dtype)


def far_kernel(count, half, lo, place_ref, q_ref, own_ref, lse_ref, *refs):
    k_refs, v_refs = refs[:count], refs[count : 2 * count]
    (out_ref,) = refs[2 * count :]
    width = out_ref.shape[1]
    rows = slice(lo, lo + out_ref.shape[0])

    @pl.when(place_ref[0] < half)
    def _():
        out_ref[...] = own_ref[rows, :width]

    @pl.when(place_ref[0] >= half)
    def _():
        for h in range(width // HD):
            at = slice(h * HD, (h + 1) * HD)
            result, lse = softmax_rows(
                q_ref[rows, at], [k[:, at] for k in k_refs], [v[:, at] for v in v_refs], [None] * count, HD**-0.5
            )
            share = 1.0 / (1.0 + jnp.exp2(lse - lse_ref[rows, h : h + 1]))
            out_ref[:, at] = mix(own_ref[rows, at], result, share, out_ref.dtype)


def project(rows, image, first, w_ref, out_ref):
    chunk = out_ref.shape[1]
    block = min(chunk, BLOCK)
    nothing = jnp.zeros_like(rows)
    text_rows, image_rows = jnp.where(image, nothing, rows), jnp.where(image, rows, nothing)
    for b in range(0, chunk, block):
        at = slice(first + b, first + b + block)
        total = jnp.dot(text_rows, w_ref[0, :, at], preferred_element_type=jnp.float32)
        total += jnp.dot(image_rows, w_ref[1, :, at], preferred_element_type=jnp.float32)
        out_ref[:, b : b + block] = total.astype(out_ref.dtype)


def merge_kernel(half, lo, first, place_ref, own_ref, lse_ref, near_ref, back_ref, kinds_ref, w_ref, att_ref, out_ref):
    count, _ = att_ref.shape
    rows = slice(lo, lo + count)
    skip, shipped = near_ref.shape[1], back_ref.shape[1] // HD
    att_ref[:, :skip] = near_ref[...]

    @pl.when(place_ref[0] < half)
    def _():
        att_ref[:, skip:] = own_ref[rows, skip:]

    @pl.when(place_ref[0] >= half)
    def _():
        terms = back_ref[count:, :count].astype(jnp.float32)
        far_lse = sum(terms[i * shipped : (i + 1) * shipped] for i in range(3))
        before = skip // HD
        far_lse = jnp.concatenate(
            [
                jnp.zeros((before, count), jnp.float32),
                far_lse,
                jnp.zeros((LANES - before - shipped, count), jnp.float32),
            ],
            axis=0,
        ).T
        mine = 1.0 / (1.0 + jnp.exp2(far_lse - lse_ref[rows, :]))
        for h in range(shipped):
            at, there = slice(h * HD, (h + 1) * HD), slice(skip + h * HD, skip + (h + 1) * HD)
            share = mine[:, before + h : before + h + 1]
            att_ref[:, there] = mix(own_ref[rows, there], back_ref[:count, at], share, att_ref.dtype)

    project(att_ref[...], kinds_ref[rows, :1] == 1, first, w_ref, out_ref)


def stream_kernel(offset, place_ref, w_hbm, kinds_ref, *refs):
    *att_refs, out_ref, w_ref, sems = refs
    copies = column_copies(place_ref, (offset,), w_hbm, w_ref, sems, 0)
    for copy in copies:
        copy.start()
    for copy in copies:
        copy.wait()
    project_kernel(0, 0, kinds_ref, w_ref, *att_refs, out_ref)


def project_kernel(lo, first, kinds_ref, w_ref, *refs):
    att_refs, out_ref = refs[:-1], refs[-1]
    rows = jnp.concatenate([x[...] for x in att_refs], axis=0)
    project(rows, kinds_ref[lo : lo + rows.shape[0], :1] == 1, first, w_ref, out_ref)


def on_device(queries, key_rows, values, modality, out_weight):
    seq_count = lax.axis_size("seq")
    tp_count = lax.axis_size("tp")
    half = seq_count // 2
    place = jnp.stack([lax.axis_index("seq"), lax.axis_index("tp")]).astype(jnp.int32)
    rows, width = queries.shape
    chunk = out_weight.shape[2] // tp_count
    vmem = pl.BlockSpec(memory_space=pltpu.VMEM)
    smem = pl.BlockSpec(memory_space=pltpu.SMEM)
    hbm = pl.BlockSpec(memory_space=pltpu.HBM)
    edges = [0, *(rows * share // SHARES[-1] for share in SHARES)]
    parts = list(zip(edges[:-1], edges[1:]))

    def xor(count, bit):
        return [(i, i ^ bit) for i in range(count)]

    order = sorted(range(tp_count), reverse=True)
    loads = [tuple(order[:-1])]
    columns = {}
    pieces = PIECES * out_weight.shape[0]

    def columns_shape(loads):
        return jax.ShapeDtypeStruct((out_weight.shape[0], width, chunk * len(loads)), out_weight.dtype)

    heads = width // HD
    shipped = heads // 2
    skip = (heads - shipped) * HD
    met = lax.ppermute(
        jnp.where(place[0] >= half, queries[:, skip:], key_rows[:, : width - skip]), "seq", xor(seq_count, half)
    )
    offsets, keys, vals = [0], [key_rows], [values]
    bit = half // 2
    while bit:
        keys = keys + [lax.ppermute(x, "seq", xor(seq_count, bit)) for x in keys]
        vals = vals + [lax.ppermute(x, "seq", xor(seq_count, bit)) for x in vals]
        offsets = offsets + [o ^ bit for o in offsets]
        bit //= 2
    count = len(offsets)

    own, own_lse, own_queries, keys[0], vals[0], kinds, columns[loads[0]] = pl.pallas_call(
        functools.partial(own_kernel, tuple(offsets), loads[0]),
        out_shape=(
            jax.ShapeDtypeStruct((rows, width), jnp.bfloat16),
            jax.ShapeDtypeStruct((rows, LANES), jnp.float32),
            jax.ShapeDtypeStruct(queries.shape, queries.dtype),
            jax.ShapeDtypeStruct(key_rows.shape, key_rows.dtype),
            jax.ShapeDtypeStruct(values.shape, values.dtype),
            jax.ShapeDtypeStruct((rows, LANES), jnp.float32),
            columns_shape(loads[0]),
        ),
        in_specs=[smem] + [hbm] * 5 + [vmem] * (2 * count - 2),
        out_specs=(vmem,) * 7,
        scratch_shapes=[pltpu.VMEM((1, rows), modality.dtype), pltpu.SemaphoreType.DMA((4 + pieces * len(loads[0]),))],
        compiler_params=params(8),
        name="own",
    )(
        place,
        *(in_hbm(x) for x in (modality.reshape(1, rows), queries, key_rows, values, out_weight)),
        *keys[1:],
        *vals[1:],
    )
    far_keys = [met]
    far_vals = [lax.ppermute(values[:, :skip], "seq", xor(seq_count, half))]
    bit = half // 2
    while bit:
        far_keys = far_keys + [lax.ppermute(x, "seq", xor(seq_count, bit)) for x in far_keys]
        far_vals = far_vals + [lax.ppermute(x, "seq", xor(seq_count, bit)) for x in far_vals]
        bit //= 2


    back, near = [], []
    for p, (lo, hi) in enumerate(parts):
        found = pl.pallas_call(
            functools.partial(cross_kernel, count, half, skip, lo),
            out_shape=jax.ShapeDtypeStruct((hi - lo + lse_rows(shipped), width - skip), jnp.bfloat16),
            in_specs=[smem] + [vmem] * (1 + 2 * count),
            out_specs=vmem,
            compiler_params=params(8),
            name="cross",
        )(place, met, *keys, *vals)
        back.append(lax.ppermute(found, "seq", [xor(seq_count, half), xor(seq_count, half)][p]))
        near.append(
            pl.pallas_call(
                functools.partial(far_kernel, count, half, lo),
                out_shape=jax.ShapeDtypeStruct((hi - lo, skip), jnp.bfloat16),
                in_specs=[smem] + [vmem] * (3 + 2 * count),
                out_specs=vmem,
                compiler_params=params(8),
                name="far",
            )(place, own_queries, own, own_lse, *far_keys, *far_vals)
        )

    def columns_of(offset):
        (held,) = (x for x in loads if offset in x)
        return columns[held], held.index(offset) * chunk

    def merged(p, offset):
        weight, first = columns_of(offset)
        lo, hi = parts[p]
        return pl.pallas_call(
            functools.partial(merge_kernel, half, lo, first),
            out_shape=(
                jax.ShapeDtypeStruct((hi - lo, width), jnp.bfloat16),
                jax.ShapeDtypeStruct((hi - lo, chunk), jnp.bfloat16),
            ),
            in_specs=[smem] + [vmem] * 6,
            out_specs=(vmem, vmem),
            compiler_params=params(8),
            name="merge",
        )(place, own, own_lse, near[p], back[p], kinds, weight)

    def streamed(attended, offset):
        return pl.pallas_call(
            functools.partial(stream_kernel, offset),
            out_shape=jax.ShapeDtypeStruct((rows, chunk), jnp.bfloat16),
            in_specs=[smem, hbm] + [vmem] * (1 + len(attended)),
            out_specs=vmem,
            scratch_shapes=[
                pltpu.VMEM((out_weight.shape[0], width, chunk), out_weight.dtype),
                pltpu.SemaphoreType.DMA((pieces,)),
            ],
            compiler_params=params(12),
            name="stream",
        )(place, in_hbm(out_weight), kinds, *attended)

    def projected(lo, attended, offset):
        weight, first = columns_of(offset)
        return pl.pallas_call(
            functools.partial(project_kernel, lo, first),
            out_shape=jax.ShapeDtypeStruct((sum(x.shape[0] for x in attended), chunk), jnp.bfloat16),
            in_specs=[vmem] * (2 + len(attended)),
            out_specs=vmem,
            compiler_params=params(8),
            name="project",
        )(kinds, weight, *attended)

    def add(*terms):
        return sum(x.astype(jnp.float32) for x in terms)

    attended, sums = [], []
    for p in range(len(parts)):
        here, first = merged(p, tp_count - 1)
        attended.append(here)
        have = {tp_count - 1: first}
        for offset in range(2, tp_count - 1):
            have[offset] = projected(parts[p][0], [here], offset)
        bit, arrivals = 1, []
        while bit < tp_count:
            keep = dict(have)
            for offset in sorted(have, reverse=True):
                if offset & bit:
                    arrived = lax.ppermute(keep.pop(offset), "tp", xor(tp_count, bit))
                    if offset == bit:
                        arrivals.append(arrived)
                    else:
                        keep[offset ^ bit] = add(have[offset ^ bit], arrived).astype(jnp.bfloat16)
            have = keep
            bit *= 2
        sums.append(arrivals)
    beside = projected(0, attended, 1)
    beside = lax.ppermute(beside, "tp", xor(tp_count, 1))
    total = streamed(attended, 0)
    total = add(total, beside)
    for arrivals in zip(*sums):
        total = add(total, jnp.concatenate(arrivals, axis=0))
    return total.astype(jnp.bfloat16)


def solution(mesh):
    in_specs = (
        P(("dp", "seq"), "tp"),
        P(("dp", "seq"), "tp"),
        P(("dp", "seq"), "tp"),
        P(("dp", "seq")),
        P(None, "tp", None),
    )
    out_specs = P(("dp", "seq"), "tp")

    return jax.shard_map(on_device, mesh=mesh, in_specs=in_specs, out_specs=out_specs, check_vma=False)
```

```python
import functools

import jax
import jax.numpy as jnp
import numpy as np
from jax import lax
from jax.experimental import pallas as pl
from jax.experimental.pallas import tpu as pltpu
from jax.sharding import PartitionSpec as P


HD = 128
LANES = 128
SHARES = (1, 2)
BLOCK = 256
SLICES = 4
PIECES = 4
LOG2E = float(np.log2(np.e))


def params(mib):
    return pltpu.CompilerParams(vmem_limit_bytes=mib * 1024 * 1024)


def in_hbm(x):
    return pltpu.with_memory_space_constraint(x, pltpu.HBM)


def softmax_rows(query, keys, values, masks, scale):
    scores = []
    for key, mask in zip(keys, masks):
        s = lax.dot_general(query, key, (((1,), (1,)), ((), ())), preferred_element_type=jnp.float32)
        scores.append(s if mask is None else jnp.where(mask, s, -jnp.inf))
    largest = functools.reduce(jnp.maximum, [jnp.max(s, axis=1, keepdims=True) for s in scores])
    total = None
    for s, value in zip(scores, values):
        weights = jnp.exp2((s - largest) * (scale * LOG2E)).astype(jnp.bfloat16)
        ones = jnp.ones((value.shape[0], LANES), jnp.bfloat16)
        part = jnp.dot(weights, jnp.concatenate([value, ones], axis=1), preferred_element_type=jnp.float32)
        total = part if total is None else total + part
    head = value.shape[1]
    sums = total[:, head : head + LANES]
    return total[:, :head] / sums, largest * (scale * LOG2E) + jnp.log2(sums[:, :1])


def column_copies(place_ref, offsets, w_hbm, w_ref, sems, first):
    kinds, depth, width = w_ref.shape
    chunk = width // len(offsets)
    piece = depth // PIECES
    copies = []
    for i, offset in enumerate(offsets):
        start = pl.multiple_of(jnp.bitwise_xor(place_ref[1], offset) * chunk, chunk)
        for kind in range(kinds):
            for rows in (pl.ds(r * piece, piece) for r in range(PIECES)):
                src = w_hbm.at[kind, rows, pl.ds(start, chunk)]
                dst = w_ref.at[kind, rows, pl.ds(i * chunk, chunk)]
                copies.append(pltpu.make_async_copy(src, dst, sems.at[first + len(copies)]))
    return copies


def own_kernel(offsets, loads, place_ref, kinds_hbm, q_hbm, k_hbm, v_hbm, w_hbm, *refs):
    others = len(offsets) - 1
    k_refs, v_refs = refs[:others], refs[others : 2 * others]
    out_ref, lse_ref, q_ref, k_ref, v_ref, columns_ref, w_ref, kinds_ref, sems = refs[2 * others :]
    pairs = [(kinds_hbm, kinds_ref), (v_hbm, v_ref), (q_hbm, q_ref), (k_hbm, k_ref)]
    copies = [pltpu.make_async_copy(src, dst, sems.at[i]) for i, (src, dst) in enumerate(pairs)]
    later = column_copies(place_ref, loads, w_hbm, w_ref, sems, len(pairs))
    for copy in copies + later:
        copy.start()
    me = place_ref[0]
    rows = q_ref.shape[0]
    for copy in copies:
        copy.wait()
    lse_ref[...] = jnp.zeros_like(lse_ref)
    columns_ref[...] = jnp.broadcast_to(kinds_ref[...].astype(jnp.float32), (LANES, rows)).T
    below = lax.broadcasted_iota(jnp.int32, (rows, rows), 0) >= lax.broadcasted_iota(jnp.int32, (rows, rows), 1)
    masks = [below if o == 0 else lax.broadcast(jnp.bitwise_xor(me, o), (rows, rows)) < me for o in offsets]
    for h in range(q_ref.shape[1] // HD):
        at = slice(h * HD, (h + 1) * HD)
        keys = [k[:, at] for k in (k_ref, *k_refs)]
        vals = [v[:, at] for v in (v_ref, *v_refs)]
        result, lse = softmax_rows(q_ref[:, at], keys, vals, masks, HD**-0.5)
        out_ref[:, at] = result.astype(out_ref.dtype)
        lse_ref[:, h : h + 1] = lse
    for copy in later:
        copy.wait()


def put_lse(found, h, shipped, lse):
    lanes = lax.broadcasted_iota(jnp.int32, found.shape, 1)
    return jnp.where(lanes % shipped == h, lse, found)


def lse_terms(found, shipped):
    lanes = lax.broadcasted_iota(jnp.int32, found.shape, 1)
    high = found.astype(jnp.bfloat16).astype(jnp.float32)
    middle = (found - high).astype(jnp.bfloat16).astype(jnp.float32)
    low = found - high - middle
    return jnp.where(lanes < shipped, high, jnp.where(lanes < 2 * shipped, middle, low))


def lse_rows(shipped):
    return -(-3 * shipped // 16) * 16


def cross_kernel(count, half, skip, lo, place_ref, q_ref, *refs):
    k_refs, v_refs = refs[:count], refs[count : 2 * count]
    (out_ref,) = refs[2 * count :]
    width = q_ref.shape[1]
    shipped = width // HD
    extra = lse_rows(shipped)
    rows = out_ref.shape[0] - extra
    out_ref[...] = jnp.zeros_like(out_ref)

    @pl.when(place_ref[0] < half)
    def _():
        found = jnp.zeros((rows, LANES), jnp.float32)
        for h in range(width // HD):
            at, there = slice(h * HD, (h + 1) * HD), slice(skip + h * HD, skip + (h + 1) * HD)
            query = q_ref[lo : lo + rows, at]
            result, lse = softmax_rows(
                query, [k[:, there] for k in k_refs], [v[:, there] for v in v_refs], [None] * count, HD**-0.5
            )
            out_ref[:rows, at] = result.astype(out_ref.dtype)
            found = put_lse(found, h, shipped, lse)
        out_ref[rows:, :rows] = lse_terms(found, shipped).T[:extra].astype(out_ref.dtype)


def mix(own, far, share, out_dtype):
    return (own.astype(jnp.float32) * share + far.astype(jnp.float32) * (1.0 - share)).astype(out_dtype)


def far_kernel(count, half, lo, place_ref, q_ref, own_ref, lse_ref, *refs):
    k_refs, v_refs = refs[:count], refs[count : 2 * count]
    (out_ref,) = refs[2 * count :]
    width = out_ref.shape[1]
    rows = slice(lo, lo + out_ref.shape[0])

    @pl.when(place_ref[0] < half)
    def _():
        out_ref[...] = own_ref[rows, :width]

    @pl.when(place_ref[0] >= half)
    def _():
        for h in range(width // HD):
            at = slice(h * HD, (h + 1) * HD)
            result, lse = softmax_rows(
                q_ref[rows, at], [k[:, at] for k in k_refs], [v[:, at] for v in v_refs], [None] * count, HD**-0.5
            )
            share = 1.0 / (1.0 + jnp.exp2(lse - lse_ref[rows, h : h + 1]))
            out_ref[:, at] = mix(own_ref[rows, at], result, share, out_ref.dtype)


def project(rows, image, first, w_ref, out_ref):
    chunk = out_ref.shape[1]
    block = min(chunk, BLOCK)
    nothing = jnp.zeros_like(rows)
    text_rows, image_rows = jnp.where(image, nothing, rows), jnp.where(image, rows, nothing)
    for b in range(0, chunk, block):
        at = slice(first + b, first + b + block)
        total = jnp.dot(text_rows, w_ref[0, :, at], preferred_element_type=jnp.float32)
        total += jnp.dot(image_rows, w_ref[1, :, at], preferred_element_type=jnp.float32)
        out_ref[:, b : b + block] = total.astype(out_ref.dtype)


def merge_kernel(half, lo, first, place_ref, own_ref, lse_ref, near_ref, back_ref, kinds_ref, w_ref, att_ref, out_ref):
    count, _ = att_ref.shape
    rows = slice(lo, lo + count)
    skip, shipped = near_ref.shape[1], back_ref.shape[1] // HD
    upper = place_ref[0] >= half
    terms = back_ref[count:, :count].astype(jnp.float32)
    far_lse = sum(terms[i * shipped : (i + 1) * shipped] for i in range(3))
    before = skip // HD
    far_lse = jnp.concatenate(
        [
            jnp.zeros((before, count), jnp.float32),
            far_lse,
            jnp.zeros((LANES - before - shipped, count), jnp.float32),
        ],
        axis=0,
    ).T
    mine = 1.0 / (1.0 + jnp.exp2(far_lse - lse_ref[rows, :]))
    pieces = [near_ref[...]]
    for h in range(shipped):
        at, there = slice(h * HD, (h + 1) * HD), slice(skip + h * HD, skip + (h + 1) * HD)
        share = mine[:, before + h : before + h + 1]
        alone = own_ref[rows, there]
        pieces.append(jnp.where(upper, mix(alone, back_ref[:count, at], share, att_ref.dtype), alone))
    merged = jnp.concatenate(pieces, axis=1)
    att_ref[...] = merged
    project(merged, kinds_ref[rows, :1] == 1, first, w_ref, out_ref)


def stream_kernel(offset, place_ref, w_hbm, kinds_ref, *refs):
    *att_refs, out_ref, w_ref, sems = refs
    copies = column_copies(place_ref, (offset,), w_hbm, w_ref, sems, 0)
    for copy in copies:
        copy.start()
    for copy in copies:
        copy.wait()
    project_kernel(0, 0, kinds_ref, w_ref, *att_refs, out_ref)


def project_kernel(lo, first, kinds_ref, w_ref, *refs):
    att_refs, out_ref = refs[:-1], refs[-1]
    rows = jnp.concatenate([x[...] for x in att_refs], axis=0)
    project(rows, kinds_ref[lo : lo + rows.shape[0], :1] == 1, first, w_ref, out_ref)


def total_kernel(parts, first_ref, second_ref, *refs):
    *arrived, out_hbm, out_ref, sems = refs
    each = len(arrived) // len(parts)
    copies = []
    for p, (lo, hi) in enumerate(parts):
        piece = (hi - lo) // SLICES
        for start in range(0, hi - lo, piece):
            rows, here = slice(lo + start, lo + start + piece), slice(start, start + piece)
            total = first_ref[rows, :].astype(jnp.float32) + second_ref[rows, :].astype(jnp.float32)
            for ref in arrived[p * each : (p + 1) * each]:
                total += ref[here, :].astype(jnp.float32)
            out_ref[rows, :] = total.astype(out_ref.dtype)
            copies.append(pltpu.make_async_copy(out_ref.at[rows], out_hbm.at[rows], sems.at[len(copies)]))
            copies[-1].start()
    for copy in copies:
        copy.wait()


def on_device(queries, key_rows, values, modality, out_weight):
    seq_count = lax.axis_size("seq")
    tp_count = lax.axis_size("tp")
    half = seq_count // 2
    place = jnp.stack([lax.axis_index("seq"), lax.axis_index("tp")]).astype(jnp.int32)
    rows, width = queries.shape
    chunk = out_weight.shape[2] // tp_count
    vmem = pl.BlockSpec(memory_space=pltpu.VMEM)
    smem = pl.BlockSpec(memory_space=pltpu.SMEM)
    hbm = pl.BlockSpec(memory_space=pltpu.HBM)
    edges = [0, *(rows * share // SHARES[-1] for share in SHARES)]
    parts = list(zip(edges[:-1], edges[1:]))

    def xor(count, bit):
        return [(i, i ^ bit) for i in range(count)]

    order = sorted(range(tp_count), reverse=True)
    loads = [tuple(order[:-1])]
    columns = {}
    pieces = PIECES * out_weight.shape[0]

    def columns_shape(loads):
        return jax.ShapeDtypeStruct((out_weight.shape[0], width, chunk * len(loads)), out_weight.dtype)

    heads = width // HD
    shipped = heads // 2
    skip = (heads - shipped) * HD
    met = lax.ppermute(
        jnp.where(place[0] >= half, queries[:, skip:], key_rows[:, : width - skip]), "seq", xor(seq_count, half)
    )
    offsets, keys, vals = [0], [key_rows], [values]
    bit = half // 2
    while bit:
        keys = keys + [lax.ppermute(x, "seq", xor(seq_count, bit)) for x in keys]
        vals = vals + [lax.ppermute(x, "seq", xor(seq_count, bit)) for x in vals]
        offsets = offsets + [o ^ bit for o in offsets]
        bit //= 2
    count = len(offsets)

    own, own_lse, own_queries, keys[0], vals[0], kinds, columns[loads[0]] = pl.pallas_call(
        functools.partial(own_kernel, tuple(offsets), loads[0]),
        out_shape=(
            jax.ShapeDtypeStruct((rows, width), jnp.bfloat16),
            jax.ShapeDtypeStruct((rows, LANES), jnp.float32),
            jax.ShapeDtypeStruct(queries.shape, queries.dtype),
            jax.ShapeDtypeStruct(key_rows.shape, key_rows.dtype),
            jax.ShapeDtypeStruct(values.shape, values.dtype),
            jax.ShapeDtypeStruct((rows, LANES), jnp.float32),
            columns_shape(loads[0]),
        ),
        in_specs=[smem] + [hbm] * 5 + [vmem] * (2 * count - 2),
        out_specs=(vmem,) * 7,
        scratch_shapes=[pltpu.VMEM((1, rows), modality.dtype), pltpu.SemaphoreType.DMA((4 + pieces * len(loads[0]),))],
        compiler_params=params(8),
        name="own",
    )(
        place,
        *(in_hbm(x) for x in (modality.reshape(1, rows), queries, key_rows, values, out_weight)),
        *keys[1:],
        *vals[1:],
    )
    far_keys = [met]
    far_vals = [lax.ppermute(values[:, :skip], "seq", xor(seq_count, half))]
    bit = half // 2
    while bit:
        far_keys = far_keys + [lax.ppermute(x, "seq", xor(seq_count, bit)) for x in far_keys]
        far_vals = far_vals + [lax.ppermute(x, "seq", xor(seq_count, bit)) for x in far_vals]
        bit //= 2


    back, near = [], []
    for p, (lo, hi) in enumerate(parts):
        found = pl.pallas_call(
            functools.partial(cross_kernel, count, half, skip, lo),
            out_shape=jax.ShapeDtypeStruct((hi - lo + lse_rows(shipped), width - skip), jnp.bfloat16),
            in_specs=[smem] + [vmem] * (1 + 2 * count),
            out_specs=vmem,
            compiler_params=params(8),
            name="cross",
        )(place, met, *keys, *vals)
        back.append(lax.ppermute(found, "seq", [xor(seq_count, half), xor(seq_count, half)][p]))
        near.append(
            pl.pallas_call(
                functools.partial(far_kernel, count, half, lo),
                out_shape=jax.ShapeDtypeStruct((hi - lo, skip), jnp.bfloat16),
                in_specs=[smem] + [vmem] * (3 + 2 * count),
                out_specs=vmem,
                compiler_params=params(8),
                name="far",
            )(place, own_queries, own, own_lse, *far_keys, *far_vals)
        )

    def columns_of(offset):
        (held,) = (x for x in loads if offset in x)
        return columns[held], held.index(offset) * chunk

    def merged(p, offset):
        weight, first = columns_of(offset)
        lo, hi = parts[p]
        return pl.pallas_call(
            functools.partial(merge_kernel, half, lo, first),
            out_shape=(
                jax.ShapeDtypeStruct((hi - lo, width), jnp.bfloat16),
                jax.ShapeDtypeStruct((hi - lo, chunk), jnp.bfloat16),
            ),
            in_specs=[smem] + [vmem] * 6,
            out_specs=(vmem, vmem),
            compiler_params=params(8),
            name="merge",
        )(place, own, own_lse, near[p], back[p], kinds, weight)

    def streamed(attended, offset):
        return pl.pallas_call(
            functools.partial(stream_kernel, offset),
            out_shape=jax.ShapeDtypeStruct((rows, chunk), jnp.bfloat16),
            in_specs=[smem, hbm] + [vmem] * (1 + len(attended)),
            out_specs=vmem,
            scratch_shapes=[
                pltpu.VMEM((out_weight.shape[0], width, chunk), out_weight.dtype),
                pltpu.SemaphoreType.DMA((pieces,)),
            ],
            compiler_params=params(12),
            name="stream",
        )(place, in_hbm(out_weight), kinds, *attended)

    def projected(lo, attended, offset):
        weight, first = columns_of(offset)
        return pl.pallas_call(
            functools.partial(project_kernel, lo, first),
            out_shape=jax.ShapeDtypeStruct((sum(x.shape[0] for x in attended), chunk), jnp.bfloat16),
            in_specs=[vmem] * (2 + len(attended)),
            out_specs=vmem,
            compiler_params=params(8),
            name="project",
        )(kinds, weight, *attended)

    def add(*terms):
        return sum(x.astype(jnp.float32) for x in terms)

    attended, sums = [], []
    for p in range(len(parts)):
        here, first = merged(p, tp_count - 1)
        attended.append(here)
        have = {tp_count - 1: first}
        for offset in range(2, tp_count - 1):
            have[offset] = projected(parts[p][0], [here], offset)
        bit, arrivals = 1, []
        while bit < tp_count:
            keep = dict(have)
            for offset in sorted(have, reverse=True):
                if offset & bit:
                    arrived = lax.ppermute(keep.pop(offset), "tp", xor(tp_count, bit))
                    if offset == bit:
                        arrivals.append(arrived)
                    else:
                        keep[offset ^ bit] = add(have[offset ^ bit], arrived).astype(jnp.bfloat16)
            have = keep
            bit *= 2
        sums.append(arrivals)
    beside = projected(0, attended, 1)
    beside = lax.ppermute(beside, "tp", xor(tp_count, 1))
    total = streamed(attended, 0)
    return pl.pallas_call(
        functools.partial(total_kernel, tuple(parts)),
        out_shape=jax.ShapeDtypeStruct((rows, chunk), jnp.bfloat16),
        in_specs=[vmem] * (2 + sum(len(x) for x in sums)),
        out_specs=pl.BlockSpec(memory_space=pltpu.HBM),
        scratch_shapes=[pltpu.VMEM((rows, chunk), jnp.bfloat16), pltpu.SemaphoreType.DMA((len(parts) * SLICES,))],
        compiler_params=params(8),
        name="total",
    )(total, beside, *(x for arrivals in sums for x in arrivals))


def solution(mesh):
    in_specs = (
        P(("dp", "seq"), "tp"),
        P(("dp", "seq"), "tp"),
        P(("dp", "seq"), "tp"),
        P(("dp", "seq")),
        P(None, "tp", None),
    )
    out_specs = P(("dp", "seq"), "tp")

    return jax.shard_map(on_device, mesh=mesh, in_specs=in_specs, out_specs=out_specs, check_vma=False)
```

```python
import functools

import jax
import jax.numpy as jnp
import numpy as np
from jax import lax
from jax.experimental import pallas as pl
from jax.experimental.pallas import tpu as pltpu
from jax.sharding import PartitionSpec as P


HD = 128
LANES = 128
SHARES = (1, 2)
BLOCK = 256
SLICES = 4
PIECES = 1
LOG2E = float(np.log2(np.e))


def params(mib):
    return pltpu.CompilerParams(vmem_limit_bytes=mib * 1024 * 1024)


def in_hbm(x):
    return pltpu.with_memory_space_constraint(x, pltpu.HBM)


def softmax_rows(query, keys, values, masks, scale):
    scores = []
    for key, mask in zip(keys, masks):
        s = lax.dot_general(query, key, (((1,), (1,)), ((), ())), preferred_element_type=jnp.float32)
        scores.append(s if mask is None else jnp.where(mask, s, -jnp.inf))
    largest = functools.reduce(jnp.maximum, [jnp.max(s, axis=1, keepdims=True) for s in scores])
    total = None
    for s, value in zip(scores, values):
        weights = jnp.exp2((s - largest) * (scale * LOG2E)).astype(jnp.bfloat16)
        ones = jnp.ones((value.shape[0], LANES), jnp.bfloat16)
        part = jnp.dot(weights, jnp.concatenate([value, ones], axis=1), preferred_element_type=jnp.float32)
        total = part if total is None else total + part
    head = value.shape[1]
    sums = total[:, head : head + LANES]
    return total[:, :head] / sums, largest * (scale * LOG2E) + jnp.log2(sums[:, :1])


def column_copies(place_ref, offsets, w_hbm, w_ref, sems, first):
    kinds, depth, width = w_ref.shape
    chunk = width // len(offsets)
    piece = depth // PIECES
    copies = []
    for i, offset in enumerate(offsets):
        start = pl.multiple_of(jnp.bitwise_xor(place_ref[1], offset) * chunk, chunk)
        for kind in range(kinds):
            for rows in (pl.ds(r * piece, piece) for r in range(PIECES)):
                src = w_hbm.at[kind, rows, pl.ds(start, chunk)]
                dst = w_ref.at[kind, rows, pl.ds(i * chunk, chunk)]
                copies.append(pltpu.make_async_copy(src, dst, sems.at[first + len(copies)]))
    return copies


def own_kernel(offsets, loads, place_ref, kinds_hbm, q_hbm, k_hbm, v_hbm, w_hbm, *refs):
    others = len(offsets) - 1
    k_refs, v_refs = refs[:others], refs[others : 2 * others]
    out_ref, lse_ref, q_ref, k_ref, v_ref, columns_ref, w_ref, kinds_ref, sems = refs[2 * others :]
    pairs = [(kinds_hbm, kinds_ref), (v_hbm, v_ref), (q_hbm, q_ref), (k_hbm, k_ref)]
    copies = [pltpu.make_async_copy(src, dst, sems.at[i]) for i, (src, dst) in enumerate(pairs)]
    later = column_copies(place_ref, loads, w_hbm, w_ref, sems, len(pairs))
    for copy in copies + later:
        copy.start()
    me = place_ref[0]
    rows = q_ref.shape[0]
    for copy in copies:
        copy.wait()
    lse_ref[...] = jnp.zeros_like(lse_ref)
    columns_ref[...] = jnp.broadcast_to(kinds_ref[...].astype(jnp.float32), (LANES, rows)).T
    below = lax.broadcasted_iota(jnp.int32, (rows, rows), 0) >= lax.broadcasted_iota(jnp.int32, (rows, rows), 1)
    masks = [below if o == 0 else lax.broadcast(jnp.bitwise_xor(me, o), (rows, rows)) < me for o in offsets]
    for h in range(q_ref.shape[1] // HD):
        at = slice(h * HD, (h + 1) * HD)
        keys = [k[:, at] for k in (k_ref, *k_refs)]
        vals = [v[:, at] for v in (v_ref, *v_refs)]
        result, lse = softmax_rows(q_ref[:, at], keys, vals, masks, HD**-0.5)
        out_ref[:, at] = result.astype(out_ref.dtype)
        lse_ref[:, h : h + 1] = lse
    for copy in later:
        copy.wait()


def put_lse(found, h, shipped, lse):
    lanes = lax.broadcasted_iota(jnp.int32, found.shape, 1)
    return jnp.where(lanes % shipped == h, lse, found)


def lse_lines(shipped, rows, width):
    lines = -(-shipped // (width // rows))
    return lines, -(-3 * lines // 8) * 8


def lse_terms(found, shipped, width):
    rows = found.shape[0]
    flat = found.T[:shipped]
    high = flat.astype(jnp.bfloat16).astype(jnp.float32)
    middle = (flat - high).astype(jnp.bfloat16).astype(jnp.float32)
    low = flat - high - middle
    lines, extra = lse_lines(shipped, rows, width)
    each, out = width // rows, []
    for term in (high, middle, low):
        for line in range(lines):
            heads = [term[h : h + 1] for h in range(line * each, min(shipped, (line + 1) * each))]
            pad = width - len(heads) * rows
            out.append(jnp.concatenate(heads + [jnp.zeros((1, pad), jnp.float32)] * bool(pad), axis=1))
    return jnp.concatenate(out + [jnp.zeros((extra - len(out), width), jnp.float32)] * (extra > len(out)), axis=0)


def cross_kernel(count, half, skip, lo, rows, place_ref, q_ref, *refs):
    k_refs, v_refs = refs[:count], refs[count : 2 * count]
    (out_ref,) = refs[2 * count :]
    width = q_ref.shape[1]
    shipped = width // HD
    out_ref[...] = jnp.zeros_like(out_ref)

    @pl.when(place_ref[0] < half)
    def _():
        found = jnp.zeros((rows, LANES), jnp.float32)
        for h in range(width // HD):
            at, there = slice(h * HD, (h + 1) * HD), slice(skip + h * HD, skip + (h + 1) * HD)
            query = q_ref[lo : lo + rows, at]
            result, lse = softmax_rows(
                query, [k[:, there] for k in k_refs], [v[:, there] for v in v_refs], [None] * count, HD**-0.5
            )
            out_ref[:rows, at] = result.astype(out_ref.dtype)
            found = put_lse(found, h, shipped, lse)
        out_ref[rows:, :] = lse_terms(found, shipped, width).astype(out_ref.dtype)


def mix(own, far, share, out_dtype):
    return (own.astype(jnp.float32) * share + far.astype(jnp.float32) * (1.0 - share)).astype(out_dtype)


def far_kernel(count, half, lo, place_ref, q_ref, own_ref, lse_ref, *refs):
    k_refs, v_refs = refs[:count], refs[count : 2 * count]
    (out_ref,) = refs[2 * count :]
    width = out_ref.shape[1]
    rows = slice(lo, lo + out_ref.shape[0])

    @pl.when(place_ref[0] < half)
    def _():
        out_ref[...] = own_ref[rows, :width]

    @pl.when(place_ref[0] >= half)
    def _():
        for h in range(width // HD):
            at = slice(h * HD, (h + 1) * HD)
            result, lse = softmax_rows(
                q_ref[rows, at], [k[:, at] for k in k_refs], [v[:, at] for v in v_refs], [None] * count, HD**-0.5
            )
            share = 1.0 / (1.0 + jnp.exp2(lse - lse_ref[rows, h : h + 1]))
            out_ref[:, at] = mix(own_ref[rows, at], result, share, out_ref.dtype)


def project(rows, image, first, w_ref, out_ref):
    chunk = out_ref.shape[1]
    block = min(chunk, BLOCK)
    nothing = jnp.zeros_like(rows)
    text_rows, image_rows = jnp.where(image, nothing, rows), jnp.where(image, rows, nothing)
    for b in range(0, chunk, block):
        at = slice(first + b, first + b + block)
        total = jnp.dot(text_rows, w_ref[0, :, at], preferred_element_type=jnp.float32)
        total += jnp.dot(image_rows, w_ref[1, :, at], preferred_element_type=jnp.float32)
        out_ref[:, b : b + block] = total.astype(out_ref.dtype)


def merge_kernel(half, lo, first, place_ref, own_ref, lse_ref, near_ref, back_ref, kinds_ref, w_ref, att_ref, out_ref):
    count, _ = att_ref.shape
    rows = slice(lo, lo + count)
    skip, shipped = near_ref.shape[1], back_ref.shape[1] // HD
    upper = place_ref[0] >= half
    lines, _ = lse_lines(shipped, count, back_ref.shape[1])
    terms = back_ref[count:, :].astype(jnp.float32)
    terms = sum(terms[i * lines : (i + 1) * lines] for i in range(3))
    each = back_ref.shape[1] // count
    far_lse = jnp.concatenate(
        [terms[h // each : h // each + 1, h % each * count : (h % each + 1) * count] for h in range(shipped)], axis=0
    )
    before = skip // HD
    far_lse = jnp.concatenate(
        [
            jnp.zeros((before, count), jnp.float32),
            far_lse,
            jnp.zeros((LANES - before - shipped, count), jnp.float32),
        ],
        axis=0,
    ).T
    mine = 1.0 / (1.0 + jnp.exp2(far_lse - lse_ref[rows, :]))
    pieces = [near_ref[...]]
    for h in range(shipped):
        at, there = slice(h * HD, (h + 1) * HD), slice(skip + h * HD, skip + (h + 1) * HD)
        share = mine[:, before + h : before + h + 1]
        alone = own_ref[rows, there]
        pieces.append(jnp.where(upper, mix(alone, back_ref[:count, at], share, att_ref.dtype), alone))
    merged = jnp.concatenate(pieces, axis=1)
    att_ref[...] = merged
    project(merged, kinds_ref[rows, :1] == 1, first, w_ref, out_ref)


def stream_kernel(offset, place_ref, w_hbm, kinds_ref, *refs):
    *att_refs, out_ref, w_ref, sems = refs
    copies = column_copies(place_ref, (offset,), w_hbm, w_ref, sems, 0)
    for copy in copies:
        copy.start()
    for copy in copies:
        copy.wait()
    project_kernel(0, 0, kinds_ref, w_ref, *att_refs, out_ref)


def project_kernel(lo, first, kinds_ref, w_ref, *refs):
    att_refs, out_ref = refs[:-1], refs[-1]
    rows = jnp.concatenate([x[...] for x in att_refs], axis=0)
    project(rows, kinds_ref[lo : lo + rows.shape[0], :1] == 1, first, w_ref, out_ref)


def total_kernel(parts, first_ref, second_ref, *refs):
    *arrived, out_hbm, out_ref, sems = refs
    each = len(arrived) // len(parts)
    copies = []
    for p, (lo, hi) in enumerate(parts):
        piece = (hi - lo) // SLICES
        for start in range(0, hi - lo, piece):
            rows, here = slice(lo + start, lo + start + piece), slice(start, start + piece)
            total = first_ref[rows, :].astype(jnp.float32) + second_ref[rows, :].astype(jnp.float32)
            for ref in arrived[p * each : (p + 1) * each]:
                total += ref[here, :].astype(jnp.float32)
            out_ref[rows, :] = total.astype(out_ref.dtype)
            copies.append(pltpu.make_async_copy(out_ref.at[rows], out_hbm.at[rows], sems.at[len(copies)]))
            copies[-1].start()
    for copy in copies:
        copy.wait()


def on_device(queries, key_rows, values, modality, out_weight):
    seq_count = lax.axis_size("seq")
    tp_count = lax.axis_size("tp")
    half = seq_count // 2
    place = jnp.stack([lax.axis_index("seq"), lax.axis_index("tp")]).astype(jnp.int32)
    rows, width = queries.shape
    chunk = out_weight.shape[2] // tp_count
    vmem = pl.BlockSpec(memory_space=pltpu.VMEM)
    smem = pl.BlockSpec(memory_space=pltpu.SMEM)
    hbm = pl.BlockSpec(memory_space=pltpu.HBM)
    edges = [0, *(rows * share // SHARES[-1] for share in SHARES)]
    parts = list(zip(edges[:-1], edges[1:]))

    def xor(count, bit):
        return [(i, i ^ bit) for i in range(count)]

    order = sorted(range(tp_count), reverse=True)
    loads = [tuple(order[:-1])]
    columns = {}
    pieces = PIECES * out_weight.shape[0]

    def columns_shape(loads):
        return jax.ShapeDtypeStruct((out_weight.shape[0], width, chunk * len(loads)), out_weight.dtype)

    heads = width // HD
    shipped = heads // 2
    skip = (heads - shipped) * HD
    met = lax.ppermute(
        jnp.where(place[0] >= half, queries[:, skip:], key_rows[:, : width - skip]), "seq", xor(seq_count, half)
    )
    offsets, keys, vals = [0], [key_rows], [values]
    bit = half // 2
    while bit:
        keys = keys + [lax.ppermute(x, "seq", xor(seq_count, bit)) for x in keys]
        vals = vals + [lax.ppermute(x, "seq", xor(seq_count, bit)) for x in vals]
        offsets = offsets + [o ^ bit for o in offsets]
        bit //= 2
    count = len(offsets)

    own, own_lse, own_queries, keys[0], vals[0], kinds, columns[loads[0]] = pl.pallas_call(
        functools.partial(own_kernel, tuple(offsets), loads[0]),
        out_shape=(
            jax.ShapeDtypeStruct((rows, width), jnp.bfloat16),
            jax.ShapeDtypeStruct((rows, LANES), jnp.float32),
            jax.ShapeDtypeStruct(queries.shape, queries.dtype),
            jax.ShapeDtypeStruct(key_rows.shape, key_rows.dtype),
            jax.ShapeDtypeStruct(values.shape, values.dtype),
            jax.ShapeDtypeStruct((rows, LANES), jnp.float32),
            columns_shape(loads[0]),
        ),
        in_specs=[smem] + [hbm] * 5 + [vmem] * (2 * count - 2),
        out_specs=(vmem,) * 7,
        scratch_shapes=[pltpu.VMEM((1, rows), modality.dtype), pltpu.SemaphoreType.DMA((4 + pieces * len(loads[0]),))],
        compiler_params=params(8),
        name="own",
    )(
        place,
        *(in_hbm(x) for x in (modality.reshape(1, rows), queries, key_rows, values, out_weight)),
        *keys[1:],
        *vals[1:],
    )
    far_keys = [met]
    far_vals = [lax.ppermute(values[:, :skip], "seq", xor(seq_count, half))]
    bit = half // 2
    while bit:
        far_keys = far_keys + [lax.ppermute(x, "seq", xor(seq_count, bit)) for x in far_keys]
        far_vals = far_vals + [lax.ppermute(x, "seq", xor(seq_count, bit)) for x in far_vals]
        bit //= 2


    back, near = [], []
    for p, (lo, hi) in enumerate(parts):
        found = pl.pallas_call(
            functools.partial(cross_kernel, count, half, skip, lo, hi - lo),
            out_shape=jax.ShapeDtypeStruct((hi - lo + lse_lines(shipped, hi - lo, width - skip)[1], width - skip), jnp.bfloat16),
            in_specs=[smem] + [vmem] * (1 + 2 * count),
            out_specs=vmem,
            compiler_params=params(8),
            name="cross",
        )(place, met, *keys, *vals)
        back.append(lax.ppermute(found, "seq", [xor(seq_count, half), xor(seq_count, half)][p]))
        near.append(
            pl.pallas_call(
                functools.partial(far_kernel, count, half, lo),
                out_shape=jax.ShapeDtypeStruct((hi - lo, skip), jnp.bfloat16),
                in_specs=[smem] + [vmem] * (3 + 2 * count),
                out_specs=vmem,
                compiler_params=params(8),
                name="far",
            )(place, own_queries, own, own_lse, *far_keys, *far_vals)
        )

    def columns_of(offset):
        (held,) = (x for x in loads if offset in x)
        return columns[held], held.index(offset) * chunk

    def merged(p, offset):
        weight, first = columns_of(offset)
        lo, hi = parts[p]
        return pl.pallas_call(
            functools.partial(merge_kernel, half, lo, first),
            out_shape=(
                jax.ShapeDtypeStruct((hi - lo, width), jnp.bfloat16),
                jax.ShapeDtypeStruct((hi - lo, chunk), jnp.bfloat16),
            ),
            in_specs=[smem] + [vmem] * 6,
            out_specs=(vmem, vmem),
            compiler_params=params(8),
            name="merge",
        )(place, own, own_lse, near[p], back[p], kinds, weight)

    def streamed(attended, offset):
        return pl.pallas_call(
            functools.partial(stream_kernel, offset),
            out_shape=jax.ShapeDtypeStruct((rows, chunk), jnp.bfloat16),
            in_specs=[smem, hbm] + [vmem] * (1 + len(attended)),
            out_specs=vmem,
            scratch_shapes=[
                pltpu.VMEM((out_weight.shape[0], width, chunk), out_weight.dtype),
                pltpu.SemaphoreType.DMA((pieces,)),
            ],
            compiler_params=params(12),
            name="stream",
        )(place, in_hbm(out_weight), kinds, *attended)

    def projected(lo, attended, offset):
        weight, first = columns_of(offset)
        return pl.pallas_call(
            functools.partial(project_kernel, lo, first),
            out_shape=jax.ShapeDtypeStruct((sum(x.shape[0] for x in attended), chunk), jnp.bfloat16),
            in_specs=[vmem] * (2 + len(attended)),
            out_specs=vmem,
            compiler_params=params(8),
            name="project",
        )(kinds, weight, *attended)

    def add(*terms):
        return sum(x.astype(jnp.float32) for x in terms)

    attended, sums = [], []
    for p in range(len(parts)):
        here, first = merged(p, tp_count - 1)
        attended.append(here)
        have = {tp_count - 1: first}
        for offset in range(2, tp_count - 1):
            have[offset] = projected(parts[p][0], [here], offset)
        bit, arrivals = 1, []
        while bit < tp_count:
            keep = dict(have)
            for offset in sorted(have, reverse=True):
                if offset & bit:
                    arrived = lax.ppermute(keep.pop(offset), "tp", xor(tp_count, bit))
                    if offset == bit:
                        arrivals.append(arrived)
                    else:
                        keep[offset ^ bit] = add(have[offset ^ bit], arrived).astype(jnp.bfloat16)
            have = keep
            bit *= 2
        sums.append(arrivals)
    beside = projected(0, attended, 1)
    beside = lax.ppermute(beside, "tp", xor(tp_count, 1))
    total = streamed(attended, 0)
    return pl.pallas_call(
        functools.partial(total_kernel, tuple(parts)),
        out_shape=jax.ShapeDtypeStruct((rows, chunk), jnp.bfloat16),
        in_specs=[vmem] * (2 + sum(len(x) for x in sums)),
        out_specs=pl.BlockSpec(memory_space=pltpu.HBM),
        scratch_shapes=[pltpu.VMEM((rows, chunk), jnp.bfloat16), pltpu.SemaphoreType.DMA((len(parts) * SLICES,))],
        compiler_params=params(8),
        name="total",
    )(total, beside, *(x for arrivals in sums for x in arrivals))


def solution(mesh):
    in_specs = (
        P(("dp", "seq"), "tp"),
        P(("dp", "seq"), "tp"),
        P(("dp", "seq"), "tp"),
        P(("dp", "seq")),
        P(None, "tp", None),
    )
    out_specs = P(("dp", "seq"), "tp")

    return jax.shard_map(on_device, mesh=mesh, in_specs=in_specs, out_specs=out_specs, check_vma=False)
```
